32 devices in a mesh: enc: 4 (over z), rep: 8 (over y, x, core).
Axes of the slice: x: 2, y: 2, z: 4, core: 2. Of those that a mesh axis runs over, the one named last changes fastest.
Arguments:
- encoder_out: bfloat16 [128, 32, 3200], P(('enc', 'rep')), may hold values from -600 to 600
- destination: int32 [1024, 1], P(('enc', 'rep')), may hold values from 0 to 3; in each aligned block of 32 rows (0 to 31, 32 to 63, ...) at most 9 rows name the same one
- norm_gain: float32 [12800], replicated, may hold values from 0.1 to 1.9
- norm_bias: float32 [12800], replicated, may hold values from -3 to 3
- cotangent: bfloat16 [1152, 12800], P(('enc', 'rep')), may hold values from -6 to 6
Outputs:
- visual_tokens: bfloat16 [1152, 12800], P(('enc', 'rep'))
- encoder_grad: bfloat16 [128, 32, 3200], P(('enc', 'rep'))
- gain_grad: float32 [12800], replicated
- bias_grad: float32 [12800], replicated
The draws below stay inside these ranges and needn't reach their ends.
Inputs may be any that keep to these rules, and one draw needn't show every extreme that they name: `destination`: in the rows of one device no owner is named by more than 9 rows, a bound that some block reaches.
All inputs are finite; a program needn't handle non-finite values.
Results may differ from the reference program's by a relative error of at most 0.001.
Values may be sent and summed in bfloat16 or wider, within the bound.
A program may use at most 64 MiB of HBM per device.

```python
import math
import jax
import jax.numpy as jnp
import numpy as np
from jax import lax

D = 3200
GRID = 32
TOK_DEV = 32
CAP = 9
PROWS_ALL = 128
TOKENS = 1024
SLOTS = 1152
N_ENC = 4
N_REP = 8
DEVICES = 32


def draw_encoder_out(key, part):
    key_base, key_rows, key_cols = jax.random.split(key, 3)
    shape = (PROWS_ALL, GRID, D)
    drawn = jnp.clip(jax.random.normal(key_base, shape, jnp.float32), -6.0, 6.0)
    row_scale = jnp.exp(jax.random.uniform(key_rows, (PROWS_ALL, GRID, 1), jnp.float32, 0.0, 2.3))
    col_scale = jnp.exp(jax.random.uniform(key_cols, (1, 1, D), jnp.float32, 0.0, 2.3))
    return (drawn * row_scale * col_scale).astype(jnp.bfloat16)


def levels(stream_key, shape, cuts, low, top_value):
    loudness, own = 1.0, jax.random.fold_in(stream_key, 6)
    for axis_at, parts in cuts:
        steps = jnp.exp(jax.random.uniform(jax.random.fold_in(own, axis_at), (parts,), jnp.float32, low / len(cuts), top_value / len(cuts)))
        loudness = loudness * jnp.repeat(steps, shape[axis_at] // parts).reshape([-1 if axis == axis_at else 1 for axis in range(len(shape))])
    return loudness


def routed_block(key, own, number, rows, number_of, top, bound, lean):
    sequence = jax.random.permutation(key, number_of)
    packed, ordinary = portions_of(number_of, rows * top, bound, lean, True), portions_of(number_of, rows * top, bound, lean, False)
    places = jnp.arange(number_of)

    def named(sizes, rotation):
        used = int((sizes > 0).sum())
        fixed = max(1, used // 4)
        moved = fixed + (places - fixed + rotation * (used - fixed)) % max(1, number_of - fixed)
        return jnp.zeros((number_of,), jnp.int32).at[sequence[jnp.where(places < fixed, places, moved)]].set(jnp.asarray(sizes, jnp.int32))

    sizes = jnp.where(number % 4 == 0, named(packed, number // 4), named(ordinary, number - number // 4 - 1))
    mixed = jax.random.permutation(jax.random.fold_in(own, 3), number_of)
    source_of, receiver = mixed[0:number_of // 2 * 2:2], mixed[1:number_of // 2 * 2:2]
    margin = jnp.minimum(sizes[source_of] - 1, bound - sizes[receiver]) // 2
    margin = jnp.where((source_of == sequence[0]) | (receiver == sequence[0]) | (sizes[receiver] == 0), 0, jnp.maximum(margin, 0))
    moved = jax.random.randint(jax.random.fold_in(own, 4), (number_of // 2,), 0, 1 << 20) % (margin + 1)
    sizes = sizes.at[source_of].add(-moved).at[receiver].add(moved)
    items = jnp.searchsorted(jnp.cumsum(sizes), jnp.arange(rows * top), side="right").astype(jnp.int32)
    listing = items.reshape(top, rows).T
    listing = listing[jax.random.permutation(jax.random.fold_in(own, 1), rows)]
    rotation = jax.random.randint(jax.random.fold_in(own, 2), (rows, 1), 0, top)
    return jnp.take_along_axis(listing, (jnp.arange(top)[None, :] + rotation) % top, axis=1)


def portions_of(number_of, total, limit, slope, full):
    weights = [(1 << 20) // math.isqrt(standing ** slope) + 1 for standing in range(1, number_of + 1)]
    largest = limit if full else min(limit, max(-(-total // number_of), total * weights[0] // sum(weights)))
    least = 1 if total - largest >= number_of - 1 else 0
    counts, rest = [largest] + [least] * (number_of - 1), total - largest - least * (number_of - 1)
    while rest > 0:
        free = [i for i in range(1, number_of) if counts[i] < largest] or [i for i in range(1, number_of) if counts[i] < limit]
        pool, budget = sum([weights[i] for i in free]), rest
        for i in free:
            more = min(limit - counts[i], max(1, budget * weights[i] // pool), rest)
            counts[i] = counts[i] + more
            rest = rest - more
    return np.array(counts)


def scatter_about(key, extent, scale, bound, shards=(), kind=jnp.bfloat16):
    drawn = jax.random.normal(key, extent, jnp.float32) * scale
    if len(shards) > 0:
        drawn = levels(key, extent, shards, -0.22, 0.18) * drawn
    return jnp.clip(drawn, min=-bound, max=bound).astype(kind)


def setup_inputs(seed: int = 0) -> dict:
    streams_of = jax.random.split(jax.random.key(seed), 6)
    encoder_out = draw_encoder_out(jax.random.fold_in(streams_of[5], 71), 0)
    destination_keys = jax.random.split(jax.random.fold_in(streams_of[1], 1), TOKENS // TOK_DEV)
    destination_turns = jax.random.permutation(jax.random.fold_in(streams_of[1], 3), TOKENS // TOK_DEV)
    destination = jax.vmap(lambda own, number: routed_block(jax.random.fold_in(streams_of[1], 2), own, number, TOK_DEV, N_ENC, 1, CAP, 2))(destination_keys, destination_turns).reshape((TOKENS, 1))
    norm_gain = jnp.clip(1.0 + 0.18 * jax.random.normal(streams_of[2], (4 * D,), jnp.float32), 0.1, 1.9)
    norm_bias = scatter_about(streams_of[3], (4 * D,), 0.5, 3.0, (), jnp.float32)
    cotangent = scatter_about(streams_of[4], (SLOTS, 4 * D), 1.0, 6.0, ((0, 32),))
    return {"encoder_out": encoder_out, "destination": destination, "norm_gain": norm_gain, "norm_bias": norm_bias, "cotangent": cotangent}


epsilon = 1e-05

def shuffle_tokens(patches):
    height, across, channels = patches.shape
    grouped = patches.reshape(height // 2, 2, across // 2, 2, channels).transpose(0, 2, 1, 3, 4)
    return grouped.reshape(height // 2 * (across // 2), 4 * channels)

def unshuffle_tokens(tokens, height, across, channels):
    grouped = tokens.reshape(height // 2, across // 2, 2, 2, channels).transpose(0, 2, 1, 3, 4)
    return grouped.reshape(height, across, channels)

def norm_forward(values, norm_gain, norm_bias):
    values = values.astype(jnp.float32)
    center = lax.optimization_barrier(jnp.mean(values, axis=-1, keepdims=True))
    spread = lax.optimization_barrier(jnp.mean(jnp.square(values - center), axis=-1, keepdims=True))
    inverse = lax.rsqrt(spread + epsilon)
    normed = (values - center) * inverse
    return (normed, inverse, normed * norm_gain + norm_bias)

def norm_backward(upstream, normed, inverse, norm_gain):
    scaled = upstream * norm_gain
    mean_grad = lax.optimization_barrier(jnp.mean(scaled, axis=-1, keepdims=True))
    mean_proj = lax.optimization_barrier(jnp.mean(scaled * normed, axis=-1, keepdims=True))
    return inverse * (scaled - mean_grad - normed * mean_proj)

def reference(encoder_out, destination, norm_gain, norm_bias, cotangent):
    height, across, channels = encoder_out.shape
    tokens = shuffle_tokens(encoder_out)
    feature_width = tokens.shape[1]
    normed, inverse, output = norm_forward(tokens, norm_gain, norm_bias)
    owners = destination[:, 0].astype(jnp.int32).reshape(DEVICES, TOK_DEV)
    onehot = (owners[:, :, None] == jnp.arange(N_ENC, dtype=jnp.int32)[None, None, :]).astype(jnp.int32)
    before = jnp.cumsum(onehot, axis=1) - onehot
    within = lax.optimization_barrier(jnp.sum(before * onehot, axis=2)).astype(jnp.int32)
    source = jnp.arange(DEVICES, dtype=jnp.int32)[:, None]
    sender = source // N_REP
    replica = source % N_REP
    target = owners * N_REP + replica
    rows_at = (target * (N_ENC * CAP) + sender * CAP + within).reshape(-1).astype(jnp.int32)
    visual = jnp.zeros((SLOTS, feature_width), jnp.bfloat16).at[rows_at].set(output.astype(jnp.bfloat16))
    upstream = cotangent[rows_at].astype(jnp.float32)
    token_grad = norm_backward(upstream, normed, inverse, norm_gain).astype(jnp.bfloat16)
    factor = 1.0 / math.sqrt(TOKENS)
    gain_grad = lax.optimization_barrier(jnp.sum(upstream * normed, axis=0)) * factor
    bias_grad = lax.optimization_barrier(jnp.sum(upstream, axis=0)) * factor
    encoder_grad = unshuffle_tokens(token_grad, height, across, channels)
    return (visual, encoder_grad, gain_grad, bias_grad)
```

```python
import functools
import math

import jax
import jax.numpy as jnp
import numpy as np
from jax import lax
from jax.experimental import pallas as pl
from jax.experimental.pallas import tpu as pltpu
from jax.sharding import PartitionSpec as P

epsilon = 1e-05
LANES = 128
QUADS = 4
PIECES = 4
F32 = jnp.float32
BF16 = jnp.bfloat16


def onehot(mask):
    return jnp.where(mask, 1.0, 0.0).astype(BF16)


def dot(a, b):
    return jnp.dot(a, b, preferred_element_type=F32)


class Sizes:
    def __init__(self, encoder_shape, slot_shape, groups, reps):
        height, across, self.channels = encoder_shape
        self.height, self.across = height, across
        self.groups, self.reps = groups, reps
        self.patches = height * across
        self.tokens = self.patches // QUADS
        self.slots = slot_shape[0]
        self.capacity = self.slots // groups
        folded = self.capacity * QUADS
        self.whole = folded // 16 * 16
        self.rest = folded - self.whole
        self.rest_rows = self.rest * PIECES
        self.rows_a = groups * self.whole
        self.rows_b = groups * self.rest_rows
        tiles = self.channels // LANES
        self.width = -(-tiles // PIECES) * LANES
        self.cuts = []
        start = 0
        while start < self.channels:
            self.cuts.append((start, min(self.width, self.channels - start)))
            start += self.width
        self.share = -(-tiles // reps) * LANES
        self.padded_slots = -(-self.slots // 16) * 16

    def codes(self):
        out = np.full((PIECES, self.rows_a + self.rows_b), -1, np.int32)
        for group in range(self.groups):
            for row in range(self.whole):
                out[:, group * self.whole + row] = group * self.capacity * QUADS + row
            for row in range(self.rest):
                for piece in range(PIECES):
                    at = self.rows_a + group * self.rest_rows + row * PIECES + piece
                    out[piece, at] = group * self.capacity * QUADS + self.whole + row
        return out

    def permutation(self):
        out = np.zeros((self.patches, self.patches), np.float32)
        half = self.across // 2
        for token in range(self.tokens):
            a, b = divmod(token, half)
            for quad in range(QUADS):
                dy, dx = divmod(quad, 2)
                out[quad * self.tokens + token, (2 * a + dy) * self.across + 2 * b + dx] = 1.0
        return out


def take(z, buffers, pick, first, width):
    a, b = buffers
    block = None
    if z.rows_a:
        block = dot(pick[:, :z.rows_a], a[:, :, first:first + width].reshape(z.rows_a, width))
    if z.rows_b:
        term = dot(pick[:, z.rows_a:], b[...].reshape(z.rows_b, z.width)[:, :width])
        block = term if block is None else block + term
    return block


def exclusive(me, d, count):
    if count & (count - 1):
        return lax.rem(me + d, count)
    bit = 1
    while bit < count:
        if d & bit:
            me = me + bit - 2 * bit * lax.rem(me // bit, 2)
        bit *= 2
    return me


def kernel(z, factor, x_hbm, own_ref, gain_ref, bias_ref, cot_hbm, perm_ref, back_ref, col_ref, row_ref,
           visual, grad_ref, fin_ref,
           x_ref, cot_ref, cs_a, cs_b, cr_a, cr_b, vs_a, vs_b, vr_a, vr_b, norm, ups, part, part_in, mid, mid_in, fin,
           cot_sem, x_sem, send_sem, recv_sem, self_sem, rs_send, rs_recv, ex_send, ex_recv, ag_send, ag_recv):
    G, N, T = z.groups, z.reps, z.tokens
    C, rows_a, rows_b = z.channels, z.rows_a, z.rows_b
    me, rep = lax.axis_index("enc"), lax.axis_index("rep")
    order = list(range(1, G))
    features = QUADS * C

    barrier = pltpu.get_barrier_semaphore()
    for d in range(1, G):
        pl.semaphore_signal(barrier, inc=1, device_id={"enc": exclusive(me, d, G)}, device_id_type=pl.DeviceIdType.MESH)
    for d in range(1, N):
        pl.semaphore_signal(barrier, inc=1, device_id={"rep": lax.rem(rep + d, N)}, device_id_type=pl.DeviceIdType.MESH)

    def cot_copy(piece, quad):
        first, width = z.cuts[piece]
        at = pl.ds(quad * C + first, width)
        return pltpu.make_async_copy(cot_hbm.at[:, at], cot_ref.at[:, at], cot_sem.at[piece, quad])

    for piece in range(len(z.cuts)):
        for quad in range(QUADS):
            cot_copy(piece, quad).start()
    x_copy = pltpu.make_async_copy(x_hbm, x_ref, x_sem)
    x_copy.start()

    def views(buffers, index, piece):
        a, b = buffers
        if piece == PIECES:
            return b.at[index]
        start, width = z.cuts[piece]
        return a.at[index, :, pl.ds(start, width)]

    def remote(which, source, target, piece, d):
        peer = exclusive(me, d, G)
        return pltpu.make_async_remote_copy(
            src_ref=views(source, peer, piece), dst_ref=views(target, me, piece),
            send_sem=send_sem.at[which, piece, d], recv_sem=recv_sem.at[which, piece, d],
            device_id={"enc": peer}, device_id_type=pl.DeviceIdType.MESH)

    def own(which, source, target, piece):
        return pltpu.make_async_copy(views(source, me, piece), views(target, me, piece), self_sem.at[which, piece])

    pieces = (list(range(len(z.cuts))) if rows_a else []) + ([PIECES] if rows_b else [])

    def start(which, source, target, piece):
        if piece not in pieces:
            return
        for d in order:
            remote(which, source, target, piece, d).start()
        own(which, source, target, piece).start()

    def arrived(which, source, target, piece):
        if piece not in pieces:
            return
        for d in order:
            remote(which, source, target, piece, d).wait_recv()
        own(which, source, target, piece).wait()

    def store_block(buffers, piece, value, rest):
        a, b = buffers
        first, width = z.cuts[piece]
        if rows_a:
            a[:, :, first:first + width] = value[:rows_a].astype(BF16).reshape(G, z.whole, width)
        if rows_b:
            more = value[rows_a:]
            if width < z.width:
                more = jnp.concatenate([more, jnp.zeros((rows_b, z.width - width), F32)], axis=1)
            return more if rest is None else rest + more
        return None

    gather_block = functools.partial(take, z)

    cot_send, cot_got, vis_send, vis_got = (cs_a, cs_b), (cr_a, cr_b), (vs_a, vs_b), (vr_a, vr_b)

    rest = None
    slot_lane = lax.broadcasted_iota(jnp.int32, (rows_a + rows_b, z.slots), 1) * QUADS
    for piece, (first, width) in enumerate(z.cuts):
        block = None
        for quad in range(QUADS):
            cot_copy(piece, quad).wait()
            pick = onehot(col_ref[:, piece:piece + 1] == slot_lane + quad)
            term = dot(pick, cot_ref[:, quad * C + first:quad * C + first + width])
            block = term if block is None else block + term
        rest = store_block(cot_send, piece, block, rest)
        if piece == 0:
            pl.semaphore_wait(barrier, G + N - 2)
        start(0, cot_send, cot_got, piece)
    if rows_b:
        cs_b[...] = rest.astype(BF16).reshape(G, z.rest_rows, z.width)
        start(0, cot_send, cot_got, PIECES)

    lane = lax.broadcasted_iota(jnp.int32, (T, QUADS * T), 1)
    token = lax.broadcasted_iota(jnp.int32, (T, QUADS * T), 0)
    quad_of = sum((lane >= n * T).astype(jnp.int32) for n in range(1, QUADS))
    token_of = lane - quad_of * T
    corner = lax.broadcasted_iota(jnp.int32, (T, T), 0) == lax.broadcasted_iota(jnp.int32, (T, T), 1)
    owner = jnp.sum(jnp.where(corner, own_ref[...].astype(F32), 0.0), axis=1, keepdims=True)
    owner_row = jnp.sum(jnp.where(token == token_of, owner, 0.0), axis=0, keepdims=True)
    rank_row = jnp.sum(jnp.where((owner == owner_row) & (token < token_of), 1.0, 0.0), axis=0, keepdims=True)
    code_row = (owner_row * z.capacity + rank_row) * QUADS + quad_of[:1].astype(F32)
    square = (QUADS * T, QUADS * T)
    eye = lax.broadcasted_iota(jnp.int32, square, 0) == lax.broadcasted_iota(jnp.int32, square, 1)
    code_col = jnp.sum(jnp.where(eye, code_row, 0.0), axis=1, keepdims=True)

    def by_token(column):
        total = column[:T]
        for quad in range(1, QUADS):
            total = total + column[quad * T:(quad + 1) * T]
        return total

    def spread(column):
        return jnp.concatenate([column] * QUADS, axis=0)

    def params(ref, first, width):
        def row(at):
            return jnp.concatenate([ref[n:n + 1, :] for n in range(at // LANES, (at + width) // LANES)], axis=1)

        return jnp.concatenate([jnp.broadcast_to(row(quad * C + first), (T, width)) for quad in range(QUADS)], axis=0)

    x_copy.wait()

    total = jnp.zeros((QUADS * T, 1), F32)
    for first, width in z.cuts:
        values = dot(perm_ref[...], x_ref[:, first:first + width])
        norm[:, first:first + width] = values
        total = total + jnp.sum(values, axis=1, keepdims=True)
    center = spread(by_token(total) / features)
    total = jnp.zeros((QUADS * T, 1), F32)
    for first, width in z.cuts:
        values = norm[:, first:first + width] - center
        total = total + jnp.sum(values * values, axis=1, keepdims=True)
    inverse = spread(lax.rsqrt(by_token(total) / features + epsilon))

    rest = None
    for piece, (first, width) in enumerate(z.cuts):
        values = (norm[:, first:first + width] - center) * inverse
        norm[:, first:first + width] = values
        output = values * params(gain_ref, first, width) + params(bias_ref, first, width)
        pick = onehot(col_ref[:, piece:piece + 1].astype(F32) == code_row)
        rest = store_block(vis_send, piece, dot(pick, output.astype(BF16)), rest)
    if rows_b:
        vs_b[...] = rest.astype(BF16).reshape(G, z.rest_rows, z.width)

    arrived(0, cot_send, cot_got, 0)
    arrived(0, cot_send, cot_got, 1)
    start(1, vis_send, vis_got, PIECES)
    start(1, vis_send, vis_got, 0)
    arrived(0, cot_send, cot_got, 2)
    arrived(0, cot_send, cot_got, 3)
    arrived(0, cot_send, cot_got, PIECES)
    start(1, vis_send, vis_got, 1)

    mean_grad = jnp.zeros((QUADS * T, 1), F32)
    mean_proj = jnp.zeros((QUADS * T, 1), F32)
    part[...] = jnp.zeros_like(part)
    for piece, (first, width) in enumerate(z.cuts):
        pick = onehot(code_col == row_ref[piece:piece + 1, :].astype(F32))
        upstream = gather_block(cot_got, pick, first, width)
        normed = norm[:, first:first + width]
        product = upstream * normed
        scale = params(gain_ref, first, width)
        scaled = upstream * scale
        ups[:, first:first + width] = scaled
        mean_grad = mean_grad + jnp.sum(scaled, axis=1, keepdims=True)
        mean_proj = mean_proj + jnp.sum(scaled * normed, axis=1, keepdims=True)
        for quad in range(QUADS):
            rows = slice(quad * T, (quad + 1) * T)
            part[quad:quad + 1, first:first + width] = jnp.sum(product[rows], axis=0, keepdims=True)
            part[QUADS + quad:QUADS + quad + 1, first:first + width] = jnp.sum(upstream[rows], axis=0, keepdims=True)

    def columns(index):
        return pl.ds(pl.multiple_of(index * z.share, LANES), z.share)

    def reduce_copy(d):
        peer = lax.rem(rep + d, N)
        return pltpu.make_async_remote_copy(
            src_ref=part.at[:, columns(peer)], dst_ref=part_in.at[rep], send_sem=rs_send.at[d], recv_sem=rs_recv.at[d],
            device_id={"rep": peer}, device_id_type=pl.DeviceIdType.MESH)

    def exchange_copy(d):
        peer = exclusive(me, d, G)
        return pltpu.make_async_remote_copy(
            src_ref=mid, dst_ref=mid_in.at[me], send_sem=ex_send.at[d], recv_sem=ex_recv.at[d],
            device_id={"enc": peer}, device_id_type=pl.DeviceIdType.MESH)

    def gather_copy(d):
        peer = lax.rem(rep + d, N)
        return pltpu.make_async_remote_copy(
            src_ref=mid, dst_ref=fin.at[rep], send_sem=ag_send.at[d], recv_sem=ag_recv.at[d],
            device_id={"rep": peer}, device_id_type=pl.DeviceIdType.MESH)

    for d in range(1, N):
        reduce_copy(d).start()
    part_in[pl.ds(rep, 1)] = part[:, columns(rep)][None]

    mean_grad = spread(by_token(mean_grad) / features)
    mean_proj = spread(by_token(mean_proj) / features)
    for first, width in z.cuts:
        grad = inverse * (ups[:, first:first + width] - mean_grad - norm[:, first:first + width] * mean_proj)
        grad_ref[:, first:first + width] = dot(back_ref[...], grad.astype(BF16)).astype(BF16)

    for d in range(1, N):
        reduce_copy(d).wait_recv()
    total = part_in[0]
    for index in range(1, N):
        total = total + part_in[index]
    mid[...] = total
    for d in order:
        exchange_copy(d).start()
    start(1, vis_send, vis_got, 2)
    start(1, vis_send, vis_got, 3)
    mid_in[pl.ds(me, 1)] = total[None]
    for d in order:
        exchange_copy(d).wait()
    total = mid_in[0]
    for index in range(1, G):
        total = total + mid_in[index]
    mid[...] = total * factor
    for d in range(1, N):
        gather_copy(d).start()
    fin[pl.ds(rep, 1)] = (total * factor)[None]

    slot_code = lax.broadcasted_iota(jnp.int32, (z.padded_slots, 1), 0) * QUADS
    code = jnp.concatenate([slot_code + quad for quad in range(QUADS)], axis=0)
    arrived(1, vis_send, vis_got, PIECES)
    for piece, (first, width) in enumerate(z.cuts):
        if piece == len(z.cuts) - 1:
            for d in range(1, N):
                gather_copy(d).wait_recv()
            fin_ref[...] = fin[...]
        arrived(1, vis_send, vis_got, piece)
        block = gather_block(vis_got, onehot(code == row_ref[piece:piece + 1, :]), first, width).astype(BF16)
        for quad in range(QUADS):
            at = quad * z.padded_slots
            visual[:, quad * C + first:quad * C + first + width] = block[at:at + z.slots]
    for d in range(1, N):
        reduce_copy(d).wait_send()
        gather_copy(d).wait_send()
    for piece in pieces:
        for d in order:
            remote(0, cot_send, cot_got, piece, d).wait_send()
            remote(1, vis_send, vis_got, piece, d).wait_send()


def place_kernel(z, visual_in, grad_in, fin_ref, visual_out, grad_out, gain_ref, bias_ref, sem_out):
    C = z.channels
    moves = [
        pltpu.make_async_copy(visual_in, visual_out, sem_out.at[0]),
        pltpu.make_async_copy(grad_in, grad_out, sem_out.at[1]),
    ]
    for move in moves:
        move.start()
    tiles = C // LANES
    for quad in range(QUADS):
        for tile in range(tiles):
            index, at = divmod(tile * LANES, z.share)
            row = quad * tiles + tile
            gain_ref[row:row + 1, :] = fin_ref[index, quad:quad + 1, at:at + LANES]
            bias_ref[row:row + 1, :] = fin_ref[index, QUADS + quad:QUADS + quad + 1, at:at + LANES]
    for move in moves:
        move.wait()


def body(encoder_out, destination, norm_gain, norm_bias, cotangent):
    groups, reps = lax.axis_size("enc"), lax.axis_size("rep")
    z = Sizes(encoder_out.shape, cotangent.shape, groups, reps)
    factor = 1.0 / math.sqrt(z.tokens * groups * reps)
    codes = z.codes()
    permutation = z.permutation()
    features = QUADS * z.channels
    rest_rows = max(z.rest_rows, 16)
    block_a, block_b = (groups, max(z.whole, 16), z.channels), (groups, rest_rows, z.width)
    vmem = pl.BlockSpec(memory_space=pltpu.VMEM)
    dma = pltpu.SemaphoreType.DMA
    share = (QUADS * 2, z.share)
    anywhere = pl.BlockSpec(memory_space=pl.ANY)
    rows = features // LANES
    table = jnp.asarray(codes)
    visual, grad, sums = pl.pallas_call(
        functools.partial(kernel, z, factor),
        out_shape=(
            pltpu.VMEM((z.slots, features), BF16),
            pltpu.VMEM((z.patches, z.channels), BF16),
            pltpu.VMEM((reps,) + share, F32),
        ),
        in_specs=[anywhere, vmem, vmem, vmem, anywhere, vmem, vmem, vmem, vmem],
        out_specs=(vmem, vmem, vmem),
        scratch_shapes=[
            pltpu.VMEM((z.patches, z.channels), BF16),
            pltpu.VMEM((z.slots, features), BF16),
        ]
        + [pltpu.VMEM(shape, BF16) for shape in (block_a, block_b) * 4]
        + [
            pltpu.VMEM((z.patches, z.channels), F32),
            pltpu.VMEM((z.patches, z.channels), F32),
            pltpu.VMEM((QUADS * 2, reps * z.share), F32),
            pltpu.VMEM((reps,) + share, F32),
            pltpu.VMEM(share, F32),
            pltpu.VMEM((groups,) + share, F32),
            pltpu.VMEM((reps,) + share, F32),
            dma((PIECES, QUADS)),
            dma,
            dma((2, PIECES + 1, groups)),
            dma((2, PIECES + 1, groups)),
            dma((2, PIECES + 1)),
            dma((reps,)),
            dma((reps,)),
            dma((groups,)),
            dma((groups,)),
            dma((reps,)),
            dma((reps,)),
        ],
        compiler_params=pltpu.CompilerParams(collective_id=0, has_side_effects=True, vmem_limit_bytes=60 * 1024 * 1024),
        name="dispatch",
    )(
        encoder_out.reshape(z.patches, z.channels),
        destination.reshape(1, z.tokens),
        norm_gain.reshape(rows, LANES),
        norm_bias.reshape(rows, LANES),
        cotangent,
        jnp.asarray(permutation, BF16),
        jnp.asarray(permutation.T, BF16),
        jnp.asarray(np.ascontiguousarray(codes.T)),
        table,
    )
    visual, grad, gain_sum, bias_sum = pl.pallas_call(
        functools.partial(place_kernel, z),
        out_shape=(
            jax.ShapeDtypeStruct((z.slots, features), BF16),
            jax.ShapeDtypeStruct((z.patches, z.channels), BF16),
            jax.ShapeDtypeStruct((rows, LANES), F32),
            jax.ShapeDtypeStruct((rows, LANES), F32),
        ),
        in_specs=[vmem, vmem, vmem],
        out_specs=(anywhere, anywhere, vmem, vmem),
        scratch_shapes=[dma((2,))],
        compiler_params=pltpu.CompilerParams(vmem_limit_bytes=16 * 1024 * 1024),
        name="place",
    )(visual, grad, sums)
    return (visual, grad.reshape(encoder_out.shape), gain_sum.reshape(features), bias_sum.reshape(features))


def solution(mesh):
    placed = (
        P(("enc", "rep"), None, None),
        P(("enc", "rep"), None),
        P(),
        P(),
        P(("enc", "rep"), None),
    )
    return jax.shard_map(
        body,
        mesh=mesh,
        in_specs=placed,
        out_specs=(P(("enc", "rep"), None), P(("enc", "rep"), None, None), P(), P()),
        check_vma=False,
    )
```

```python
import functools
import math

import jax
import jax.numpy as jnp
import numpy as np
from jax import lax
from jax.experimental import pallas as pl
from jax.experimental.pallas import tpu as pltpu
from jax.sharding import PartitionSpec as P

epsilon = 1e-05
LANES = 128
QUADS = 4
PIECES = 4
F32 = jnp.float32
BF16 = jnp.bfloat16


def onehot(mask):
    return jnp.where(mask, 1.0, 0.0).astype(BF16)


def dot(a, b):
    return jnp.dot(a, b, preferred_element_type=F32)


class Sizes:
    def __init__(self, encoder_shape, slot_shape, groups, reps):
        height, across, self.channels = encoder_shape
        self.height, self.across = height, across
        self.groups, self.reps = groups, reps
        self.patches = height * across
        self.tokens = self.patches // QUADS
        self.slots = slot_shape[0]
        self.capacity = self.slots // groups
        folded = self.capacity * QUADS
        self.whole = folded // 16 * 16
        self.rest = folded - self.whole
        self.rest_rows = self.rest * PIECES
        self.rows_a = groups * self.whole
        self.rows_b = groups * self.rest_rows
        tiles = self.channels // LANES
        self.width = -(-tiles // PIECES) * LANES
        self.cuts = []
        start = 0
        while start < self.channels:
            self.cuts.append((start, min(self.width, self.channels - start)))
            start += self.width
        self.share = -(-tiles // reps) * LANES
        self.padded_slots = -(-self.slots // 16) * 16

    def codes(self):
        out = np.full((PIECES, self.rows_a + self.rows_b), -1, np.int32)
        for group in range(self.groups):
            for row in range(self.whole):
                out[:, group * self.whole + row] = group * self.capacity * QUADS + row
            for row in range(self.rest):
                for piece in range(PIECES):
                    at = self.rows_a + group * self.rest_rows + row * PIECES + piece
                    out[piece, at] = group * self.capacity * QUADS + self.whole + row
        return out

    def permutation(self):
        out = np.zeros((self.patches, self.patches), np.float32)
        half = self.across // 2
        for token in range(self.tokens):
            a, b = divmod(token, half)
            for quad in range(QUADS):
                dy, dx = divmod(quad, 2)
                out[quad * self.tokens + token, (2 * a + dy) * self.across + 2 * b + dx] = 1.0
        return out


def take(z, buffers, pick, first, width):
    a, b = buffers
    block = None
    if z.rows_a:
        block = dot(pick[:, :z.rows_a], a[:, :, first:first + width].reshape(z.rows_a, width))
    if z.rows_b:
        term = dot(pick[:, z.rows_a:], b[...].reshape(z.rows_b, z.width)[:, :width])
        block = term if block is None else block + term
    return block


def exclusive(me, d, count):
    if count & (count - 1):
        return lax.rem(me + d, count)
    bit = 1
    while bit < count:
        if d & bit:
            me = me + bit - 2 * bit * lax.rem(me // bit, 2)
        bit *= 2
    return me


def nearest(me, k):
    return jnp.where(k < me, me - 1 - k, k + 1)


def kernel(z, factor, x_hbm, own_hbm, gain_hbm, bias_hbm, cot_hbm, perm_hbm, back_hbm, col_hbm, row_hbm,
           visual, grad_ref, gain_out, bias_out,
           own_ref, gain_ref, bias_ref, perm_ref, back_ref, col_ref, row_ref, x_ref, cot_ref, cs_a, cs_b, cr_a, cr_b, vs_a, vs_b, vr_a, vr_b, norm, ups, part, part_in, mid, mid_in, fin,
           here_enc, here_rep, in_sem, cot_sem, x_sem, send_sem, recv_sem, self_sem, rs_send, rs_recv, ex_send, ex_recv, ag_send, ag_recv):
    G, N, T = z.groups, z.reps, z.tokens
    C, rows_a, rows_b = z.channels, z.rows_a, z.rows_b
    me, rep = lax.axis_index("enc"), lax.axis_index("rep")
    order = list(range(1, G))
    features = QUADS * C

    barrier = pltpu.get_barrier_semaphore()

    def greet(semaphore, axis, count, at, later):
        for index in range(1, count) if later else range(count - 1):
            @pl.when(index > at if later else index < at)
            def _():
                pl.semaphore_signal(semaphore, inc=1, device_id={axis: index}, device_id_type=pl.DeviceIdType.MESH)

    greet(barrier, "enc", G, me, True)
    greet(barrier, "rep", N, rep, True)

    def cot_copy(piece, quad):
        first, width = z.cuts[piece]
        at = pl.ds(quad * C + first, width)
        return pltpu.make_async_copy(cot_hbm.at[:, at], cot_ref.at[:, at], cot_sem.at[piece, quad])

    small = [
        pltpu.make_async_copy(source, target, in_sem.at[n])
        for n, (source, target) in enumerate((
            (col_hbm, col_ref), (perm_hbm, perm_ref), (own_hbm, own_ref), (gain_hbm, gain_ref),
            (bias_hbm, bias_ref), (row_hbm, row_ref), (back_hbm, back_ref)))
    ]
    small[0].start()
    for quad in range(QUADS):
        cot_copy(0, quad).start()

    @pl.when(me + rep > 0)
    def _():
        pl.semaphore_wait(barrier, me + rep)

    greet(here_enc.at[me], "enc", G, me, False)
    greet(here_rep, "rep", N, rep, False)
    for piece in range(1, len(z.cuts)):
        for quad in range(QUADS):
            cot_copy(piece, quad).start()
    x_copy = pltpu.make_async_copy(x_hbm, x_ref, x_sem)
    x_copy.start()
    for copy in small[1:]:
        copy.start()

    def views(buffers, index, piece):
        a, b = buffers
        if piece == PIECES:
            return b.at[index]
        start, width = z.cuts[piece]
        return a.at[index, :, pl.ds(start, width)]

    def remote(which, source, target, piece, peer, sender):
        return pltpu.make_async_remote_copy(
            src_ref=views(source, peer, piece), dst_ref=views(target, sender, piece),
            send_sem=send_sem.at[which, piece, peer], recv_sem=recv_sem.at[which, piece, sender],
            device_id={"enc": peer}, device_id_type=pl.DeviceIdType.MESH)

    def own(which, source, target, piece):
        return pltpu.make_async_copy(views(source, me, piece), views(target, me, piece), self_sem.at[which, piece])

    pieces = (list(range(len(z.cuts))) if rows_a else []) + ([PIECES] if rows_b else [])

    def start(which, source, target, piece):
        if piece not in pieces:
            return
        for d in order:
            remote(which, source, target, piece, exclusive(me, d, G), me).start()
        own(which, source, target, piece).start()

    met = []

    def start_first(piece):
        if met or piece not in pieces:
            start(0, cot_send, cot_got, piece)
            return
        met.append(piece)
        for k in range(G - 1):
            peer = nearest(me, k)

            @pl.when(peer > me)
            def _():
                pl.semaphore_wait(here_enc.at[peer], 1)

            remote(0, cot_send, cot_got, piece, peer, me).start()
        own(0, cot_send, cot_got, piece).start()

    def arrived(which, source, target, piece):
        if piece not in pieces:
            return
        for d in order:
            peer = exclusive(me, d, G)
            remote(which, source, target, piece, peer, peer).wait_recv()
        own(which, source, target, piece).wait()

    def store_block(buffers, piece, value, rest):
        a, b = buffers
        first, width = z.cuts[piece]
        if rows_a:
            a[:, :, first:first + width] = value[:rows_a].astype(BF16).reshape(G, z.whole, width)
        if rows_b:
            more = value[rows_a:]
            if width < z.width:
                more = jnp.concatenate([more, jnp.zeros((rows_b, z.width - width), F32)], axis=1)
            return more if rest is None else rest + more
        return None

    gather_block = functools.partial(take, z)

    cot_send, cot_got, vis_send, vis_got = (cs_a, cs_b), (cr_a, cr_b), (vs_a, vs_b), (vr_a, vr_b)

    rest = None
    small[0].wait()
    slot_lane = lax.broadcasted_iota(jnp.int32, (rows_a + rows_b, z.slots), 1) * QUADS
    for piece, (first, width) in enumerate(z.cuts):
        block = None
        for quad in range(QUADS):
            cot_copy(piece, quad).wait()
            pick = onehot(col_ref[:, piece:piece + 1] == slot_lane + quad)
            term = dot(pick, cot_ref[:, quad * C + first:quad * C + first + width])
            block = term if block is None else block + term
        rest = store_block(cot_send, piece, block, rest)
        start_first(piece)
    if rows_b:
        cs_b[...] = rest.astype(BF16).reshape(G, z.rest_rows, z.width)
        start_first(PIECES)

    for copy in small[1:]:
        copy.wait()
    lane = lax.broadcasted_iota(jnp.int32, (T, QUADS * T), 1)
    token = lax.broadcasted_iota(jnp.int32, (T, QUADS * T), 0)
    quad_of = sum((lane >= n * T).astype(jnp.int32) for n in range(1, QUADS))
    token_of = lane - quad_of * T
    corner = lax.broadcasted_iota(jnp.int32, (T, T), 0) == lax.broadcasted_iota(jnp.int32, (T, T), 1)
    owner = jnp.sum(jnp.where(corner, own_ref[...].astype(F32), 0.0), axis=1, keepdims=True)
    owner_row = jnp.sum(jnp.where(token == token_of, owner, 0.0), axis=0, keepdims=True)
    rank_row = jnp.sum(jnp.where((owner == owner_row) & (token < token_of), 1.0, 0.0), axis=0, keepdims=True)
    code_row = (owner_row * z.capacity + rank_row) * QUADS + quad_of[:1].astype(F32)
    square = (QUADS * T, QUADS * T)
    eye = lax.broadcasted_iota(jnp.int32, square, 0) == lax.broadcasted_iota(jnp.int32, square, 1)
    code_col = jnp.sum(jnp.where(eye, code_row, 0.0), axis=1, keepdims=True)

    def by_token(column):
        total = column[:T]
        for quad in range(1, QUADS):
            total = total + column[quad * T:(quad + 1) * T]
        return total

    def spread(column):
        return jnp.concatenate([column] * QUADS, axis=0)

    def params(ref, first, width):
        def row(at):
            return jnp.concatenate([ref[n:n + 1, :] for n in range(at // LANES, (at + width) // LANES)], axis=1)

        return jnp.concatenate([jnp.broadcast_to(row(quad * C + first), (T, width)) for quad in range(QUADS)], axis=0)

    x_copy.wait()

    total = jnp.zeros((QUADS * T, 1), F32)
    for first, width in z.cuts:
        values = dot(perm_ref[...], x_ref[:, first:first + width])
        norm[:, first:first + width] = values
        total = total + jnp.sum(values, axis=1, keepdims=True)
    center = spread(by_token(total) / features)
    total = jnp.zeros((QUADS * T, 1), F32)
    for first, width in z.cuts:
        values = norm[:, first:first + width] - center
        total = total + jnp.sum(values * values, axis=1, keepdims=True)
    inverse = spread(lax.rsqrt(by_token(total) / features + epsilon))

    rest = None
    for piece, (first, width) in enumerate(z.cuts):
        values = (norm[:, first:first + width] - center) * inverse
        norm[:, first:first + width] = values
        output = values * params(gain_ref, first, width) + params(bias_ref, first, width)
        pick = onehot(col_ref[:, piece:piece + 1].astype(F32) == code_row)
        rest = store_block(vis_send, piece, dot(pick, output.astype(BF16)), rest)
    if rows_b:
        vs_b[...] = rest.astype(BF16).reshape(G, z.rest_rows, z.width)

    arrived(0, cot_send, cot_got, 0)
    arrived(0, cot_send, cot_got, 1)
    start(1, vis_send, vis_got, PIECES)
    start(1, vis_send, vis_got, 0)
    arrived(0, cot_send, cot_got, 2)
    arrived(0, cot_send, cot_got, 3)
    arrived(0, cot_send, cot_got, PIECES)
    start(1, vis_send, vis_got, 1)

    mean_grad = jnp.zeros((QUADS * T, 1), F32)
    mean_proj = jnp.zeros((QUADS * T, 1), F32)
    part[...] = jnp.zeros_like(part)
    for piece, (first, width) in enumerate(z.cuts):
        pick = onehot(code_col == row_ref[piece:piece + 1, :].astype(F32))
        upstream = gather_block(cot_got, pick, first, width)
        normed = norm[:, first:first + width]
        product = upstream * normed
        scale = params(gain_ref, first, width)
        scaled = upstream * scale
        ups[:, first:first + width] = scaled
        mean_grad = mean_grad + jnp.sum(scaled, axis=1, keepdims=True)
        mean_proj = mean_proj + jnp.sum(scaled * normed, axis=1, keepdims=True)
        for quad in range(QUADS):
            rows = slice(quad * T, (quad + 1) * T)
            part[quad:quad + 1, first:first + width] = jnp.sum(product[rows], axis=0, keepdims=True)
            part[QUADS + quad:QUADS + quad + 1, first:first + width] = jnp.sum(upstream[rows], axis=0, keepdims=True)

    def columns(index):
        return pl.ds(pl.multiple_of(index * z.share, LANES), z.share)

    def reduce_copy(d):
        peer = lax.rem(rep + d, N)
        return pltpu.make_async_remote_copy(
            src_ref=part.at[:, columns(peer)], dst_ref=part_in.at[rep], send_sem=rs_send.at[d], recv_sem=rs_recv.at[d],
            device_id={"rep": peer}, device_id_type=pl.DeviceIdType.MESH)

    def exchange_copy(d):
        peer = exclusive(me, d, G)
        return pltpu.make_async_remote_copy(
            src_ref=mid, dst_ref=mid_in.at[me], send_sem=ex_send.at[d], recv_sem=ex_recv.at[d],
            device_id={"enc": peer}, device_id_type=pl.DeviceIdType.MESH)

    def gather_copy(d):
        peer = lax.rem(rep + d, N)
        return pltpu.make_async_remote_copy(
            src_ref=mid, dst_ref=fin.at[rep], send_sem=ag_send.at[d], recv_sem=ag_recv.at[d],
            device_id={"rep": peer}, device_id_type=pl.DeviceIdType.MESH)


    @pl.when(rep < N - 1)
    def _():
        pl.semaphore_wait(here_rep, N - 1 - rep)

    for d in range(1, N):
        reduce_copy(d).start()
    part_in[pl.ds(rep, 1)] = part[:, columns(rep)][None]

    mean_grad = spread(by_token(mean_grad) / features)
    mean_proj = spread(by_token(mean_proj) / features)
    for first, width in z.cuts:
        grad = inverse * (ups[:, first:first + width] - mean_grad - norm[:, first:first + width] * mean_proj)
        grad_ref[:, first:first + width] = dot(back_ref[...], grad.astype(BF16)).astype(BF16)

    for d in range(1, N):
        reduce_copy(d).wait_recv()
    total = part_in[0]
    for index in range(1, N):
        total = total + part_in[index]
    mid[...] = total
    for d in order:
        exchange_copy(d).start()
    start(1, vis_send, vis_got, 2)
    start(1, vis_send, vis_got, 3)
    mid_in[pl.ds(me, 1)] = total[None]
    for d in order:
        exchange_copy(d).wait()
    total = mid_in[0]
    for index in range(1, G):
        total = total + mid_in[index]
    mid[...] = total * factor
    for d in range(1, N):
        gather_copy(d).start()
    fin[pl.ds(rep, 1)] = (total * factor)[None]

    slot_code = lax.broadcasted_iota(jnp.int32, (z.padded_slots, 1), 0) * QUADS
    code = jnp.concatenate([slot_code + quad for quad in range(QUADS)], axis=0)
    arrived(1, vis_send, vis_got, PIECES)
    for piece, (first, width) in enumerate(z.cuts):
        if piece == len(z.cuts) - 1:
            for d in range(1, N):
                gather_copy(d).wait_recv()
            tiles = C // LANES
            for quad in range(QUADS):
                for tile in range(tiles):
                    index, at = divmod(tile * LANES, z.share)
                    row = quad * tiles + tile
                    gain_out[row:row + 1, :] = fin[index, quad:quad + 1, at:at + LANES]
                    bias_out[row:row + 1, :] = fin[index, QUADS + quad:QUADS + quad + 1, at:at + LANES]
        arrived(1, vis_send, vis_got, piece)
        block = gather_block(vis_got, onehot(code == row_ref[piece:piece + 1, :]), first, width).astype(BF16)
        for quad in range(QUADS):
            at = quad * z.padded_slots
            visual[:, quad * C + first:quad * C + first + width] = block[at:at + z.slots]
    for d in range(1, N):
        reduce_copy(d).wait_send()
        gather_copy(d).wait_send()
    for piece in pieces:
        for d in order:
            peer = exclusive(me, d, G)
            remote(0, cot_send, cot_got, piece, peer, me).wait_send()
            remote(1, vis_send, vis_got, piece, peer, me).wait_send()


def place_kernel(*refs):
    count = (len(refs) - 1) // 2
    moves = [pltpu.make_async_copy(refs[n], refs[count + n], refs[-1].at[n]) for n in range(count)]
    for move in moves:
        move.start()
    for move in moves:
        move.wait()


def body(encoder_out, destination, norm_gain, norm_bias, cotangent):
    groups, reps = lax.axis_size("enc"), lax.axis_size("rep")
    z = Sizes(encoder_out.shape, cotangent.shape, groups, reps)
    factor = 1.0 / math.sqrt(z.tokens * groups * reps)
    codes = z.codes()
    permutation = z.permutation()
    features = QUADS * z.channels
    rest_rows = max(z.rest_rows, 16)
    block_a, block_b = (groups, max(z.whole, 16), z.channels), (groups, rest_rows, z.width)
    vmem = pl.BlockSpec(memory_space=pltpu.VMEM)
    dma = pltpu.SemaphoreType.DMA
    share = (QUADS * 2, z.share)
    anywhere = pl.BlockSpec(memory_space=pl.ANY)
    rows = features // LANES
    table = jnp.asarray(codes)
    small = [
        pltpu.VMEM((1, z.tokens), jnp.int32),
        pltpu.VMEM((rows, LANES), F32),
        pltpu.VMEM((rows, LANES), F32),
        pltpu.VMEM(permutation.shape, BF16),
        pltpu.VMEM(permutation.shape, BF16),
        pltpu.VMEM(codes.T.shape, jnp.int32),
        pltpu.VMEM(codes.shape, jnp.int32),
    ]
    results = pl.pallas_call(
        functools.partial(kernel, z, factor),
        out_shape=(
            pltpu.VMEM((z.slots, features), BF16),
            pltpu.VMEM((z.patches, z.channels), BF16),
            pltpu.VMEM((rows, LANES), F32),
            pltpu.VMEM((rows, LANES), F32),
        ),
        in_specs=[anywhere] * 9,
        out_specs=(vmem,) * 4,
        scratch_shapes=small + [
            pltpu.VMEM((z.patches, z.channels), BF16),
            pltpu.VMEM((z.slots, features), BF16),
        ]
        + [pltpu.VMEM(shape, BF16) for shape in (block_a, block_b) * 4]
        + [
            pltpu.VMEM((z.patches, z.channels), F32),
            pltpu.VMEM((z.patches, z.channels), F32),
            pltpu.VMEM((QUADS * 2, reps * z.share), F32),
            pltpu.VMEM((reps,) + share, F32),
            pltpu.VMEM(share, F32),
            pltpu.VMEM((groups,) + share, F32),
            pltpu.VMEM((reps,) + share, F32),
            pltpu.SemaphoreType.REGULAR((groups,)),
            pltpu.SemaphoreType.REGULAR,
            dma((len(small),)),
            dma((PIECES, QUADS)),
            dma,
            dma((2, PIECES + 1, groups)),
            dma((2, PIECES + 1, groups)),
            dma((2, PIECES + 1)),
            dma((reps,)),
            dma((reps,)),
            dma((groups,)),
            dma((groups,)),
            dma((reps,)),
            dma((reps,)),
        ],
        compiler_params=pltpu.CompilerParams(collective_id=0, has_side_effects=True, vmem_limit_bytes=60 * 1024 * 1024),
        name="dispatch",
    )(
        encoder_out.reshape(z.patches, z.channels),
        destination.reshape(1, z.tokens),
        norm_gain.reshape(rows, LANES),
        norm_bias.reshape(rows, LANES),
        cotangent,
        jnp.asarray(permutation, BF16),
        jnp.asarray(permutation.T, BF16),
        jnp.asarray(np.ascontiguousarray(codes.T)),
        table,
    )
    visual, grad, gain_sum, bias_sum = pl.pallas_call(
        place_kernel,
        out_shape=tuple(jax.ShapeDtypeStruct(result.shape, result.dtype) for result in results),
        in_specs=[vmem] * 4,
        out_specs=(anywhere,) * 4,
        scratch_shapes=[dma((4,))],
        compiler_params=pltpu.CompilerParams(vmem_limit_bytes=16 * 1024 * 1024),
        name="place",
    )(*results)
    return (visual, grad.reshape(encoder_out.shape), gain_sum.reshape(features), bias_sum.reshape(features))


def solution(mesh):
    placed = (
        P(("enc", "rep"), None, None),
        P(("enc", "rep"), None),
        P(),
        P(),
        P(("enc", "rep"), None),
    )
    return jax.shard_map(
        body,
        mesh=mesh,
        in_specs=placed,
        out_specs=(P(("enc", "rep"), None), P(("enc", "rep"), None, None), P(), P()),
        check_vma=False,
    )
```

```python
import functools
import math

import jax
import jax.numpy as jnp
import numpy as np
from jax import lax
from jax.experimental import pallas as pl
from jax.experimental.pallas import tpu as pltpu
from jax.sharding import PartitionSpec as P

epsilon = 1e-05
LANES = 128
QUADS = 4
PIECES = 4
F32 = jnp.float32
BF16 = jnp.bfloat16


def onehot(mask):
    return jnp.where(mask, 1.0, 0.0).astype(BF16)


def dot(a, b):
    return jnp.dot(a, b, preferred_element_type=F32)


class Sizes:
    def __init__(self, encoder_shape, slot_shape, groups, reps):
        height, across, self.channels = encoder_shape
        self.height, self.across = height, across
        self.groups, self.reps = groups, reps
        self.patches = height * across
        self.tokens = self.patches // QUADS
        self.slots = slot_shape[0]
        self.capacity = self.slots // groups
        folded = self.capacity * QUADS
        self.whole = folded // 16 * 16
        self.rest = folded - self.whole
        self.rest_rows = self.rest * PIECES
        self.rows_a = groups * self.whole
        self.rows_b = groups * self.rest_rows
        tiles = self.channels // LANES
        self.width = -(-tiles // PIECES) * LANES
        self.cuts = []
        start, width = 0, self.channels - (-(-self.channels // self.width) - 1) * self.width
        while start < self.channels:
            self.cuts.append((start, width))
            start, width = start + width, self.width
        self.share = -(-tiles // reps) * LANES
        self.shares = -(-self.channels // self.share)
        self.padded_slots = -(-self.slots // 16) * 16

    def codes(self):
        out = np.full((PIECES, self.rows_a + self.rows_b), -1, np.int32)
        for group in range(self.groups):
            for row in range(self.whole):
                out[:, group * self.whole + row] = group * self.capacity * QUADS + row
            for row in range(self.rest):
                for piece in range(PIECES):
                    at = self.rows_a + group * self.rest_rows + row * PIECES + piece
                    out[piece, at] = group * self.capacity * QUADS + self.whole + row
        return out

    def permutation(self):
        out = np.zeros((self.patches, self.patches), np.float32)
        half = self.across // 2
        for token in range(self.tokens):
            a, b = divmod(token, half)
            for quad in range(QUADS):
                dy, dx = divmod(quad, 2)
                out[quad * self.tokens + token, (2 * a + dy) * self.across + 2 * b + dx] = 1.0
        return out


def take(z, buffers, pick, first, width):
    a, b = buffers
    block = None
    if z.rows_a:
        block = dot(pick[:, :z.rows_a], a[:, :, first:first + width].reshape(z.rows_a, width))
    if z.rows_b:
        term = dot(pick[:, z.rows_a:], b[...].reshape(z.rows_b, z.width)[:, :width])
        block = term if block is None else block + term
    return block


def exclusive(me, d, count):
    if count & (count - 1):
        return lax.rem(me + d, count)
    bit = 1
    while bit < count:
        if d & bit:
            me = me + bit - 2 * bit * lax.rem(me // bit, 2)
        bit *= 2
    return me


def nearest(me, k):
    return jnp.where(k < me, me - 1 - k, k + 1)


def kernel(z, factor, x_hbm, own_hbm, gain_hbm, bias_hbm, cot_hbm, perm_hbm, back_hbm, col_hbm, row_hbm,
           visual, grad_ref, gain_out, bias_out,
           own_ref, gain_ref, bias_ref, perm_ref, back_ref, col_ref, row_ref, x_ref, cot_ref, cs_a, cs_b, cr_a, cr_b, vs_a, vs_b, vr_a, vr_b, norm, ups, part, part_in, mid, mid_in, fin,
           here_enc, here_rep, in_sem, cot_sem, x_sem, send_sem, recv_sem, self_sem, rs_send, rs_recv, ex_send, ex_recv, ag_send, ag_recv):
    G, N, T = z.groups, z.reps, z.tokens
    C, rows_a, rows_b = z.channels, z.rows_a, z.rows_b
    me, rep = lax.axis_index("enc"), lax.axis_index("rep")
    order = list(range(1, G))
    features = QUADS * C

    barrier = pltpu.get_barrier_semaphore()

    def greet(semaphore, axis, count, at, later):
        for index in range(1, count) if later else range(count - 1):
            @pl.when(index > at if later else index < at)
            def _():
                pl.semaphore_signal(semaphore, inc=1, device_id={axis: index}, device_id_type=pl.DeviceIdType.MESH)

    greet(barrier, "enc", G, me, True)
    greet(barrier, "rep", N, rep, True)

    def cot_copy(piece, quad):
        first, width = z.cuts[piece]
        at = pl.ds(quad * C + first, width)
        return pltpu.make_async_copy(cot_hbm.at[:, at], cot_ref.at[:, at], cot_sem.at[piece, quad])

    small = [
        pltpu.make_async_copy(source, target, in_sem.at[n])
        for n, (source, target) in enumerate((
            (col_hbm, col_ref), (perm_hbm, perm_ref), (own_hbm, own_ref), (gain_hbm, gain_ref),
            (bias_hbm, bias_ref), (row_hbm, row_ref), (back_hbm, back_ref)))
    ]
    small[0].start()
    for quad in range(QUADS):
        cot_copy(0, quad).start()

    @pl.when(me + rep > 0)
    def _():
        pl.semaphore_wait(barrier, me + rep)

    greet(here_enc.at[me], "enc", G, me, False)
    greet(here_rep, "rep", N, rep, False)
    for piece in range(1, len(z.cuts)):
        for quad in range(QUADS):
            cot_copy(piece, quad).start()
    x_copy = pltpu.make_async_copy(x_hbm, x_ref, x_sem)
    x_copy.start()
    for copy in small[1:]:
        copy.start()

    def views(buffers, index, piece):
        a, b = buffers
        if piece == PIECES:
            return b.at[index]
        start, width = z.cuts[piece]
        return a.at[index, :, pl.ds(start, width)]

    def remote(which, source, target, piece, peer, sender):
        return pltpu.make_async_remote_copy(
            src_ref=views(source, peer, piece), dst_ref=views(target, sender, piece),
            send_sem=send_sem.at[which, piece, peer], recv_sem=recv_sem.at[which, piece, sender],
            device_id={"enc": peer}, device_id_type=pl.DeviceIdType.MESH)

    def own(which, source, target, piece):
        return pltpu.make_async_copy(views(source, me, piece), views(target, me, piece), self_sem.at[which, piece])

    pieces = (list(range(len(z.cuts))) if rows_a else []) + ([PIECES] if rows_b else [])

    def start(which, source, target, piece):
        if piece not in pieces:
            return
        for d in order:
            remote(which, source, target, piece, exclusive(me, d, G), me).start()
        own(which, source, target, piece).start()

    met = []

    def start_first(piece):
        if met or piece not in pieces:
            start(0, cot_send, cot_got, piece)
            return
        met.append(piece)
        for k in range(G - 1):
            peer = nearest(me, k)

            @pl.when(peer > me)
            def _():
                pl.semaphore_wait(here_enc.at[peer], 1)

            remote(0, cot_send, cot_got, piece, peer, me).start()
        own(0, cot_send, cot_got, piece).start()

    def arrived(which, source, target, piece):
        if piece not in pieces:
            return
        for d in order:
            peer = exclusive(me, d, G)
            remote(which, source, target, piece, peer, peer).wait_recv()
        own(which, source, target, piece).wait()

    def store_block(buffers, piece, value, rest):
        a, b = buffers
        first, width = z.cuts[piece]
        if rows_a:
            a[:, :, first:first + width] = value[:rows_a].astype(BF16).reshape(G, z.whole, width)
        if rows_b:
            more = value[rows_a:]
            if width < z.width:
                more = jnp.concatenate([more, jnp.zeros((rows_b, z.width - width), F32)], axis=1)
            return more if rest is None else rest + more
        return None

    gather_block = functools.partial(take, z)

    cot_send, cot_got, vis_send, vis_got = (cs_a, cs_b), (cr_a, cr_b), (vs_a, vs_b), (vr_a, vr_b)

    rest = None
    count = len(z.cuts)
    ahead = min(2, count)
    small[0].wait()
    slot_lane = lax.broadcasted_iota(jnp.int32, (rows_a + rows_b, z.slots), 1) * QUADS
    for piece, (first, width) in enumerate(z.cuts):
        block = None
        for quad in range(QUADS):
            cot_copy(piece, quad).wait()
            pick = onehot(col_ref[:, piece:piece + 1] == slot_lane + quad)
            term = dot(pick, cot_ref[:, quad * C + first:quad * C + first + width])
            block = term if block is None else block + term
        rest = store_block(cot_send, piece, block, rest)
        if piece < ahead:
            start_first(piece)
    if rows_b:
        cs_b[...] = rest.astype(BF16).reshape(G, z.rest_rows, z.width)
        start_first(PIECES)
    for piece in range(ahead, count):
        start_first(piece)

    for copy in small[1:]:
        copy.wait()
    lane = lax.broadcasted_iota(jnp.int32, (T, QUADS * T), 1)
    token = lax.broadcasted_iota(jnp.int32, (T, QUADS * T), 0)
    quad_of = sum((lane >= n * T).astype(jnp.int32) for n in range(1, QUADS))
    token_of = lane - quad_of * T
    corner = lax.broadcasted_iota(jnp.int32, (T, T), 0) == lax.broadcasted_iota(jnp.int32, (T, T), 1)
    owner = jnp.sum(jnp.where(corner, own_ref[...].astype(F32), 0.0), axis=1, keepdims=True)
    owner_row = jnp.sum(jnp.where(token == token_of, owner, 0.0), axis=0, keepdims=True)
    rank_row = jnp.sum(jnp.where((owner == owner_row) & (token < token_of), 1.0, 0.0), axis=0, keepdims=True)
    code_row = (owner_row * z.capacity + rank_row) * QUADS + quad_of[:1].astype(F32)
    square = (QUADS * T, QUADS * T)
    eye = lax.broadcasted_iota(jnp.int32, square, 0) == lax.broadcasted_iota(jnp.int32, square, 1)
    code_col = jnp.sum(jnp.where(eye, code_row, 0.0), axis=1, keepdims=True)

    def by_token(column):
        total = column[:T]
        for quad in range(1, QUADS):
            total = total + column[quad * T:(quad + 1) * T]
        return total

    def spread(column):
        return jnp.concatenate([column] * QUADS, axis=0)

    def params(ref, first, width):
        def row(at):
            return jnp.concatenate([ref[n:n + 1, :] for n in range(at // LANES, (at + width) // LANES)], axis=1)

        return jnp.concatenate([jnp.broadcast_to(row(quad * C + first), (T, width)) for quad in range(QUADS)], axis=0)

    x_copy.wait()

    total = jnp.zeros((QUADS * T, 1), F32)
    for first, width in z.cuts:
        values = dot(perm_ref[...], x_ref[:, first:first + width])
        norm[:, first:first + width] = values
        total = total + jnp.sum(values, axis=1, keepdims=True)
    center = spread(by_token(total) / features)
    total = jnp.zeros((QUADS * T, 1), F32)
    for first, width in z.cuts:
        values = norm[:, first:first + width] - center
        total = total + jnp.sum(values * values, axis=1, keepdims=True)
    inverse = spread(lax.rsqrt(by_token(total) / features + epsilon))

    rest = None
    for piece, (first, width) in enumerate(z.cuts):
        values = (norm[:, first:first + width] - center) * inverse
        norm[:, first:first + width] = values
        output = values * params(gain_ref, first, width) + params(bias_ref, first, width)
        pick = onehot(col_ref[:, piece:piece + 1].astype(F32) == code_row)
        rest = store_block(vis_send, piece, dot(pick, output.astype(BF16)), rest)
    if rows_b:
        vs_b[...] = rest.astype(BF16).reshape(G, z.rest_rows, z.width)
    early, late = list(range(1, count - 1)), [count - 1, 0]
    start(1, vis_send, vis_got, PIECES)
    for piece in early:
        start(1, vis_send, vis_got, piece)

    def reduce_copy(index, sender):
        return pltpu.make_async_remote_copy(
            src_ref=part.at[:, pl.ds(index * z.share, z.share)], dst_ref=part_in.at[sender],
            send_sem=rs_send.at[index], recv_sem=rs_recv.at[sender],
            device_id={"rep": index}, device_id_type=pl.DeviceIdType.MESH)

    def exchange_copy(d):
        peer = exclusive(me, d, G)
        return pltpu.make_async_remote_copy(
            src_ref=mid, dst_ref=mid_in.at[me], send_sem=ex_send.at[d], recv_sem=ex_recv.at[d],
            device_id={"enc": peer}, device_id_type=pl.DeviceIdType.MESH)

    def gather_copy(peer, sender):
        return pltpu.make_async_remote_copy(
            src_ref=mid, dst_ref=fin.at[sender], send_sem=ag_send.at[peer], recv_sem=ag_recv.at[sender],
            device_id={"rep": peer}, device_id_type=pl.DeviceIdType.MESH)

    def others(count, act):
        for index in range(count):
            @pl.when(rep != index)
            def _():
                act(index)

    mean_grad = jnp.zeros((QUADS * T, 1), F32)
    mean_proj = jnp.zeros((QUADS * T, 1), F32)
    if N * z.share > C:
        part[:, C:] = jnp.zeros((2 * QUADS, N * z.share - C), F32)
    arrived(0, cot_send, cot_got, 0)
    if ahead > 1:
        arrived(0, cot_send, cot_got, 1)
    arrived(0, cot_send, cot_got, PIECES)
    sent = 0
    for piece, (first, width) in enumerate(z.cuts):
        if piece >= ahead:
            arrived(0, cot_send, cot_got, piece)
        pick = onehot(code_col == row_ref[piece:piece + 1, :].astype(F32))
        upstream = gather_block(cot_got, pick, first, width)
        normed = norm[:, first:first + width]
        product = upstream * normed
        scale = params(gain_ref, first, width)
        scaled = upstream * scale
        ups[:, first:first + width] = scaled
        mean_grad = mean_grad + jnp.sum(scaled, axis=1, keepdims=True)
        mean_proj = mean_proj + jnp.sum(scaled * normed, axis=1, keepdims=True)
        part[:, first:first + width] = jnp.concatenate(
            [jnp.sum(value[quad * T:(quad + 1) * T], axis=0, keepdims=True)
             for value in (product, upstream) for quad in range(QUADS)], axis=0)
        done = z.shares if piece == count - 1 else (first + width) // z.share
        if sent == 0 and done:
            @pl.when(rep < N - 1)
            def _():
                pl.semaphore_wait(here_rep, N - 1 - rep)
        for index in range(sent, done):
            @pl.when(rep != index)
            def _():
                reduce_copy(index, rep).start()

            @pl.when(rep == index)
            def _():
                part_in[index] = part[:, index * z.share:(index + 1) * z.share]
        sent = done

    @pl.when(rep < z.shares)
    def _():
        others(N, lambda index: reduce_copy(0, index).wait_recv())
        total = part_in[0]
        for index in range(1, N):
            total = total + part_in[index]
        mid[...] = total
        for d in order:
            exchange_copy(d).start()
        mid_in[pl.ds(me, 1)] = total[None]

    for piece in late:
        start(1, vis_send, vis_got, piece)

    mean_grad = spread(by_token(mean_grad) / features)
    mean_proj = spread(by_token(mean_proj) / features)
    for first, width in z.cuts:
        grad = inverse * (ups[:, first:first + width] - mean_grad - norm[:, first:first + width] * mean_proj)
        grad_ref[:, first:first + width] = dot(back_ref[...], grad.astype(BF16)).astype(BF16)

    @pl.when(rep < z.shares)
    def _():
        for d in order:
            exchange_copy(d).wait()
        total = mid_in[0]
        for index in range(1, G):
            total = total + mid_in[index]
        mid[...] = total * factor
        others(N, lambda index: gather_copy(index, rep).start())
        fin[pl.ds(rep, 1)] = (total * factor)[None]

    slot_code = lax.broadcasted_iota(jnp.int32, (z.padded_slots, 1), 0) * QUADS
    code = jnp.concatenate([slot_code + quad for quad in range(QUADS)], axis=0)
    arrived(1, vis_send, vis_got, PIECES)
    for piece in early + late:
        first, width = z.cuts[piece]
        if piece == late[-1]:
            others(z.shares, lambda index: gather_copy(0, index).wait_recv())
            tiles = C // LANES
            for quad in range(QUADS):
                for tile in range(tiles):
                    index, at = divmod(tile * LANES, z.share)
                    row = quad * tiles + tile
                    gain_out[row:row + 1, :] = fin[index, quad:quad + 1, at:at + LANES]
                    bias_out[row:row + 1, :] = fin[index, QUADS + quad:QUADS + quad + 1, at:at + LANES]
        arrived(1, vis_send, vis_got, piece)
        block = gather_block(vis_got, onehot(code == row_ref[piece:piece + 1, :]), first, width).astype(BF16)
        for quad in range(QUADS):
            at = quad * z.padded_slots
            visual[:, quad * C + first:quad * C + first + width] = block[at:at + z.slots]
    others(z.shares, lambda index: reduce_copy(index, rep).wait_send())

    @pl.when(rep < z.shares)
    def _():
        others(N, lambda index: gather_copy(index, rep).wait_send())

    for piece in pieces:
        for d in order:
            peer = exclusive(me, d, G)
            remote(0, cot_send, cot_got, piece, peer, me).wait_send()
            remote(1, vis_send, vis_got, piece, peer, me).wait_send()


def place_kernel(*refs):
    count = (len(refs) - 1) // 2
    moves = [pltpu.make_async_copy(refs[n], refs[count + n], refs[-1].at[n]) for n in range(count)]
    for move in moves:
        move.start()
    for move in moves:
        move.wait()


def body(encoder_out, destination, norm_gain, norm_bias, cotangent):
    groups, reps = lax.axis_size("enc"), lax.axis_size("rep")
    z = Sizes(encoder_out.shape, cotangent.shape, groups, reps)
    factor = 1.0 / math.sqrt(z.tokens * groups * reps)
    codes = z.codes()
    permutation = z.permutation()
    features = QUADS * z.channels
    rest_rows = max(z.rest_rows, 16)
    block_a, block_b = (groups, max(z.whole, 16), z.channels), (groups, rest_rows, z.width)
    vmem = pl.BlockSpec(memory_space=pltpu.VMEM)
    dma = pltpu.SemaphoreType.DMA
    share = (QUADS * 2, z.share)
    anywhere = pl.BlockSpec(memory_space=pl.ANY)
    rows = features // LANES
    table = jnp.asarray(codes)
    small = [
        pltpu.VMEM((1, z.tokens), jnp.int32),
        pltpu.VMEM((rows, LANES), F32),
        pltpu.VMEM((rows, LANES), F32),
        pltpu.VMEM(permutation.shape, BF16),
        pltpu.VMEM(permutation.shape, BF16),
        pltpu.VMEM(codes.T.shape, jnp.int32),
        pltpu.VMEM(codes.shape, jnp.int32),
    ]
    results = pl.pallas_call(
        functools.partial(kernel, z, factor),
        out_shape=(
            pltpu.VMEM((z.slots, features), BF16),
            pltpu.VMEM((z.patches, z.channels), BF16),
            pltpu.VMEM((rows, LANES), F32),
            pltpu.VMEM((rows, LANES), F32),
        ),
        in_specs=[anywhere] * 9,
        out_specs=(vmem,) * 4,
        scratch_shapes=small + [
            pltpu.VMEM((z.patches, z.channels), BF16),
            pltpu.VMEM((z.slots, features), BF16),
        ]
        + [pltpu.VMEM(shape, BF16) for shape in (block_a, block_b) * 4]
        + [
            pltpu.VMEM((z.patches, z.channels), F32),
            pltpu.VMEM((z.patches, z.channels), F32),
            pltpu.VMEM((QUADS * 2, reps * z.share), F32),
            pltpu.VMEM((reps,) + share, F32),
            pltpu.VMEM(share, F32),
            pltpu.VMEM((groups,) + share, F32),
            pltpu.VMEM((reps,) + share, F32),
            pltpu.SemaphoreType.REGULAR((groups,)),
            pltpu.SemaphoreType.REGULAR,
            dma((len(small),)),
            dma((PIECES, QUADS)),
            dma,
            dma((2, PIECES + 1, groups)),
            dma((2, PIECES + 1, groups)),
            dma((2, PIECES + 1)),
            dma((reps,)),
            dma((reps,)),
            dma((groups,)),
            dma((groups,)),
            dma((reps,)),
            dma((reps,)),
        ],
        compiler_params=pltpu.CompilerParams(collective_id=0, has_side_effects=True, vmem_limit_bytes=60 * 1024 * 1024),
        name="dispatch",
    )(
        encoder_out.reshape(z.patches, z.channels),
        destination.reshape(1, z.tokens),
        norm_gain.reshape(rows, LANES),
        norm_bias.reshape(rows, LANES),
        cotangent,
        jnp.asarray(permutation, BF16),
        jnp.asarray(permutation.T, BF16),
        jnp.asarray(np.ascontiguousarray(codes.T)),
        table,
    )
    visual, grad, gain_sum, bias_sum = pl.pallas_call(
        place_kernel,
        out_shape=tuple(jax.ShapeDtypeStruct(result.shape, result.dtype) for result in results),
        in_specs=[vmem] * 4,
        out_specs=(anywhere,) * 4,
        scratch_shapes=[dma((4,))],
        compiler_params=pltpu.CompilerParams(vmem_limit_bytes=16 * 1024 * 1024),
        name="place",
    )(*results)
    return (visual, grad.reshape(encoder_out.shape), gain_sum.reshape(features), bias_sum.reshape(features))


def solution(mesh):
    placed = (
        P(("enc", "rep"), None, None),
        P(("enc", "rep"), None),
        P(),
        P(),
        P(("enc", "rep"), None),
    )
    return jax.shard_map(
        body,
        mesh=mesh,
        in_specs=placed,
        out_specs=(P(("enc", "rep"), None), P(("enc", "rep"), None, None), P(), P()),
        check_vma=False,
    )
```

```python
import functools
import math

import jax
import jax.numpy as jnp
import numpy as np
from jax import lax
from jax.experimental import pallas as pl
from jax.experimental.pallas import tpu as pltpu
from jax.sharding import PartitionSpec as P

epsilon = 1e-05
LANES = 128
QUADS = 4
PIECES = 4
F32 = jnp.float32
BF16 = jnp.bfloat16


def onehot(mask):
    return jnp.where(mask, 1.0, 0.0).astype(BF16)


def dot(a, b):
    return jnp.dot(a, b, preferred_element_type=F32)


class Sizes:
    def __init__(self, encoder_shape, slot_shape, groups, reps):
        height, across, self.channels = encoder_shape
        self.height, self.across = height, across
        self.groups, self.reps = groups, reps
        self.patches = height * across
        self.tokens = self.patches // QUADS
        self.slots = slot_shape[0]
        self.capacity = self.slots // groups
        folded = self.capacity * QUADS
        self.whole = folded // 16 * 16
        self.rest = folded - self.whole
        self.rest_rows = self.rest * PIECES
        self.rows_a = groups * self.whole
        self.rows_b = groups * self.rest_rows
        tiles = self.channels // LANES
        self.width = -(-tiles // PIECES) * LANES
        self.cuts = []
        start, width = 0, self.channels - (-(-self.channels // self.width) - 1) * self.width
        while start < self.channels:
            self.cuts.append((start, width))
            start, width = start + width, self.width
        self.tiles = tiles
        self.base, self.extra = divmod(tiles, reps)
        self.share = -(-tiles // reps) * LANES
        self.padded_slots = -(-self.slots // 16) * 16

    def codes(self):
        out = np.full((PIECES, self.rows_a + self.rows_b), -1, np.int32)
        for group in range(self.groups):
            for row in range(self.whole):
                out[:, group * self.whole + row] = group * self.capacity * QUADS + row
            for row in range(self.rest):
                for piece in range(PIECES):
                    at = self.rows_a + group * self.rest_rows + row * PIECES + piece
                    out[piece, at] = group * self.capacity * QUADS + self.whole + row
        return out

    def permutation(self):
        out = np.zeros((self.patches, self.patches), np.float32)
        half = self.across // 2
        for token in range(self.tokens):
            a, b = divmod(token, half)
            for quad in range(QUADS):
                dy, dx = divmod(quad, 2)
                out[quad * self.tokens + token, (2 * a + dy) * self.across + 2 * b + dx] = 1.0
        return out


def take(z, buffers, pick, first, width):
    a, b = buffers
    block = None
    if z.rows_a:
        block = dot(pick[:, :z.rows_a], a[:, :, first:first + width].reshape(z.rows_a, width))
    if z.rows_b:
        term = dot(pick[:, z.rows_a:], b[...].reshape(z.rows_b, z.width)[:, :width])
        block = term if block is None else block + term
    return block


def exclusive(me, d, count):
    if count & (count - 1):
        return lax.rem(me + d, count)
    bit = 1
    while bit < count:
        if d & bit:
            me = me + bit - 2 * bit * lax.rem(me // bit, 2)
        bit *= 2
    return me


def nearest(me, k):
    return jnp.where(k < me, me - 1 - k, k + 1)


def kernel(z, factor, x_hbm, own_hbm, gain_hbm, bias_hbm, cot_hbm, perm_hbm, back_hbm, col_hbm, row_hbm,
           visual, grad_ref, gain_out, bias_out,
           own_ref, gain_ref, bias_ref, perm_ref, back_ref, col_ref, row_ref, x_ref, cot_ref, cs_a, cs_b, cr_a, cr_b, vs_a, vs_b, vr_a, vr_b, norm, ups, part, part_in, mid, mid_in, fin,
           here_enc, here_rep, in_sem, cot_sem, x_sem, send_sem, recv_sem, self_sem, rs_send, rs_recv, ex_send, ex_recv, ag_send, ag_recv):
    G, N, T = z.groups, z.reps, z.tokens
    C, rows_a, rows_b = z.channels, z.rows_a, z.rows_b
    me, rep = lax.axis_index("enc"), lax.axis_index("rep")
    order = list(range(1, G))
    features = QUADS * C

    barrier = pltpu.get_barrier_semaphore()

    def twin(index):
        return index + 1 - 2 * lax.rem(index, 2) if N % 2 == 0 else index

    def greet(semaphore, axis, count, at, later):
        for place in range(1, count) if later else range(count - 2, -1, -1):
            @pl.when(place > at if later else place < at)
            def _():
                index = twin(place) if axis == "rep" else place
                pl.semaphore_signal(semaphore, inc=1, device_id={axis: index}, device_id_type=pl.DeviceIdType.MESH)

    rank = twin(rep)
    parted = [z.cuts[0], (z.cuts[0][1], C - z.cuts[0][1])] if len(z.cuts) > 1 else [z.cuts[0]]

    def cot_copy(half, quad):
        first, width = parted[half]
        at = pl.ds(quad * C + first, width)
        return pltpu.make_async_copy(cot_hbm.at[:, at], cot_ref.at[:, at], cot_sem.at[half, quad])

    small = [
        pltpu.make_async_copy(source, target, in_sem.at[n])
        for n, (source, target) in enumerate((
            (col_hbm, col_ref), (perm_hbm, perm_ref), (own_hbm, own_ref), (gain_hbm, gain_ref),
            (bias_hbm, bias_ref), (row_hbm, row_ref), (back_hbm, back_ref)))
    ]
    x_copy = pltpu.make_async_copy(x_hbm, x_ref, x_sem)
    small[0].start()
    for quad in range(QUADS):
        cot_copy(0, quad).start()
    greet(barrier, "enc", G, me, True)
    greet(barrier, "rep", N, rank, True)

    @pl.when(me + rank > 0)
    def _():
        pl.semaphore_wait(barrier, me + rank)

    greet(here_enc.at[me], "enc", G, me, False)
    for quad in range(QUADS):
        for half in range(1, len(parted)):
            cot_copy(half, quad).start()

    def views(buffers, index, piece):
        a, b = buffers
        if piece == PIECES:
            return b.at[index]
        start, width = z.cuts[piece]
        return a.at[index, :, pl.ds(start, width)]

    def remote(which, source, target, piece, peer, sender):
        return pltpu.make_async_remote_copy(
            src_ref=views(source, peer, piece), dst_ref=views(target, sender, piece),
            send_sem=send_sem.at[which, piece, peer], recv_sem=recv_sem.at[which, piece, sender],
            device_id={"enc": peer}, device_id_type=pl.DeviceIdType.MESH)

    def own(which, source, target, piece):
        return pltpu.make_async_copy(views(source, me, piece), views(target, me, piece), self_sem.at[which, piece])

    pieces = (list(range(len(z.cuts))) if rows_a else []) + ([PIECES] if rows_b else [])

    def start(which, source, target, *chosen):
        chosen = [piece for piece in chosen if piece in pieces]
        for d in order:
            for piece in chosen:
                remote(which, source, target, piece, exclusive(me, d, G), me).start()
        for piece in chosen:
            own(which, source, target, piece).start()

    def start_first(piece, near):
        if piece not in pieces:
            return
        for k in range(min(2, G - 1)) if near else range(2, G - 1):
            peer = nearest(me, k)

            @pl.when(peer > me)
            def _():
                pl.semaphore_wait(here_enc.at[peer], 1)

            remote(0, cot_send, cot_got, piece, peer, me).start()
        if near:
            own(0, cot_send, cot_got, piece).start()

    def arrived(which, source, target, piece):
        if piece not in pieces:
            return
        for d in order:
            peer = exclusive(me, d, G)
            remote(which, source, target, piece, peer, peer).wait_recv()
        own(which, source, target, piece).wait()

    def store_block(buffers, piece, value, rest):
        a, b = buffers
        first, width = z.cuts[piece]
        if rows_a:
            a[:, :, first:first + width] = value[:rows_a].astype(BF16).reshape(G, z.whole, width)
        if rows_b:
            more = value[rows_a:]
            if width < z.width:
                more = jnp.concatenate([more, jnp.zeros((rows_b, z.width - width), F32)], axis=1)
            return more if rest is None else rest + more
        return None

    gather_block = functools.partial(take, z)

    cot_send, cot_got, vis_send, vis_got = (cs_a, cs_b), (cr_a, cr_b), (vs_a, vs_b), (vr_a, vr_b)

    rest = None
    count = len(z.cuts)
    ahead = min(2, count)
    lead = 0 if rows_a else PIECES
    small[0].wait()
    slot_lane = lax.broadcasted_iota(jnp.int32, (rows_a + rows_b, z.slots), 1) * QUADS
    for piece, (first, width) in enumerate(z.cuts):
        block = None
        picks = [onehot(col_ref[:, piece:piece + 1] == slot_lane + quad) for quad in range(QUADS)]
        for quad in range(QUADS):
            if piece < 2:
                cot_copy(piece, quad).wait()
            term = dot(picks[quad], cot_ref[:, quad * C + first:quad * C + first + width])
            block = term if block is None else block + term
        rest = store_block(cot_send, piece, block, rest)
        if piece == lead:
            start_first(lead, True)
        if piece == ahead - 1 and lead == 0:
            start_first(lead, False)
        if 0 < piece < ahead:
            start(0, cot_send, cot_got, piece)
        if piece == 0:
            greet(here_rep, "rep", N, rank, False)
            x_copy.start()
            for copy in small[1:]:
                copy.start()
    if rows_b:
        cs_b[...] = rest.astype(BF16).reshape(G, z.rest_rows, z.width)
        if lead == PIECES:
            start_first(lead, True)
            start_first(lead, False)
        else:
            start(0, cot_send, cot_got, PIECES)
    for piece in range(ahead, count):
        start(0, cot_send, cot_got, piece)

    for copy in small[1:]:
        copy.wait()
    lane = lax.broadcasted_iota(jnp.int32, (T, QUADS * T), 1)
    token = lax.broadcasted_iota(jnp.int32, (T, QUADS * T), 0)
    quad_of = sum((lane >= n * T).astype(jnp.int32) for n in range(1, QUADS))
    token_of = lane - quad_of * T
    corner = lax.broadcasted_iota(jnp.int32, (T, T), 0) == lax.broadcasted_iota(jnp.int32, (T, T), 1)
    owner = jnp.sum(jnp.where(corner, own_ref[...].astype(F32), 0.0), axis=1, keepdims=True)
    owner_row = jnp.sum(jnp.where(token == token_of, owner, 0.0), axis=0, keepdims=True)
    rank_row = jnp.sum(jnp.where((owner == owner_row) & (token < token_of), 1.0, 0.0), axis=0, keepdims=True)
    code_row = (owner_row * z.capacity + rank_row) * QUADS + quad_of[:1].astype(F32)
    square = (QUADS * T, QUADS * T)
    eye = lax.broadcasted_iota(jnp.int32, square, 0) == lax.broadcasted_iota(jnp.int32, square, 1)
    code_col = jnp.sum(jnp.where(eye, code_row, 0.0), axis=1, keepdims=True)

    def by_token(column):
        total = column[:T]
        for quad in range(1, QUADS):
            total = total + column[quad * T:(quad + 1) * T]
        return total

    def spread(column):
        return jnp.concatenate([column] * QUADS, axis=0)

    def params(ref, first, width):
        def row(at):
            return jnp.concatenate([ref[n:n + 1, :] for n in range(at // LANES, (at + width) // LANES)], axis=1)

        return jnp.concatenate([jnp.broadcast_to(row(quad * C + first), (T, width)) for quad in range(QUADS)], axis=0)

    x_copy.wait()

    total = jnp.zeros((QUADS * T, 1), F32)
    for first, width in z.cuts:
        values = dot(perm_ref[...], x_ref[:, first:first + width])
        norm[:, first:first + width] = values
        total = total + jnp.sum(values, axis=1, keepdims=True)
    center = spread(by_token(total) / features)
    total = jnp.zeros((QUADS * T, 1), F32)
    for first, width in z.cuts:
        values = norm[:, first:first + width] - center
        total = total + jnp.sum(values * values, axis=1, keepdims=True)
    inverse = spread(lax.rsqrt(by_token(total) / features + epsilon))

    rest = None
    for piece, (first, width) in enumerate(z.cuts):
        values = (norm[:, first:first + width] - center) * inverse
        norm[:, first:first + width] = values
        output = values * params(gain_ref, first, width) + params(bias_ref, first, width)
        pick = onehot(col_ref[:, piece:piece + 1].astype(F32) == code_row)
        rest = store_block(vis_send, piece, dot(pick, output.astype(BF16)), rest)
    if rows_b:
        vs_b[...] = rest.astype(BF16).reshape(G, z.rest_rows, z.width)
    early, late = list(range(1, count - 1)), [count - 1, 0][-count:]
    start(1, vis_send, vis_got, PIECES)
    for piece in early:
        start(1, vis_send, vis_got, piece)

    def lanes(tile):
        return pl.ds(tile * LANES, LANES)

    def reduce_copy(tile, sender):
        slot, index = divmod(tile, N)
        return pltpu.make_async_remote_copy(
            src_ref=part.at[:, lanes(tile)], dst_ref=part_in.at[sender, :, lanes(slot)],
            send_sem=rs_send.at[tile], recv_sem=rs_recv.at[slot, sender],
            device_id={"rep": index}, device_id_type=pl.DeviceIdType.MESH)

    def held(index):
        return z.base + (index < z.extra)

    def holding(act):
        if z.extra:
            @pl.when(rep < z.extra)
            def _():
                act(z.base + 1)

        if z.base:
            @pl.when(rep >= z.extra)
            def _():
                act(z.base)

    def exchange_copy(d, count):
        peer = exclusive(me, d, G)
        at = pl.ds(0, count * LANES)
        return pltpu.make_async_remote_copy(
            src_ref=mid.at[:, at], dst_ref=mid_in.at[me, :, at], send_sem=ex_send.at[d], recv_sem=ex_recv.at[d],
            device_id={"enc": peer}, device_id_type=pl.DeviceIdType.MESH)

    def gather_copy(peer, sender, count):
        at = pl.ds(0, count * LANES)
        return pltpu.make_async_remote_copy(
            src_ref=mid.at[:, at], dst_ref=fin.at[sender, :, at], send_sem=ag_send.at[peer], recv_sem=ag_recv.at[sender],
            device_id={"rep": peer}, device_id_type=pl.DeviceIdType.MESH)

    def others(count, act):
        for index in range(count):
            @pl.when(rep != index)
            def _():
                act(index)

    mean_grad = jnp.zeros((QUADS * T, 1), F32)
    mean_proj = jnp.zeros((QUADS * T, 1), F32)
    arrived(0, cot_send, cot_got, 0)
    if ahead > 1:
        arrived(0, cot_send, cot_got, 1)
    arrived(0, cot_send, cot_got, PIECES)
    sent = 0
    for piece, (first, width) in enumerate(z.cuts):
        if piece >= ahead:
            arrived(0, cot_send, cot_got, piece)
        pick = onehot(code_col == row_ref[piece:piece + 1, :].astype(F32))
        upstream = gather_block(cot_got, pick, first, width)
        normed = norm[:, first:first + width]
        product = upstream * normed
        scale = params(gain_ref, first, width)
        scaled = upstream * scale
        ups[:, first:first + width] = scaled
        mean_grad = mean_grad + jnp.sum(scaled, axis=1, keepdims=True)
        mean_proj = mean_proj + jnp.sum(scaled * normed, axis=1, keepdims=True)
        part[:, first:first + width] = jnp.concatenate(
            [jnp.sum(value[quad * T:(quad + 1) * T], axis=0, keepdims=True)
             for value in (product, upstream) for quad in range(QUADS)], axis=0)
        done = (first + width) // LANES
        if sent == 0:
            @pl.when(rank < N - 1)
            def _():
                pl.semaphore_wait(here_rep, N - 1 - rank)
        for tile in range(sent, done):
            slot, index = divmod(tile, N)

            @pl.when(rep != index)
            def _():
                reduce_copy(tile, rep).start()

            @pl.when(rep == index)
            def _():
                part_in[index, :, slot * LANES:(slot + 1) * LANES] = part[:, tile * LANES:(tile + 1) * LANES]
        sent = done

    @holding
    def _(count):
        at = slice(0, count * LANES)
        for slot in range(count):
            others(N, lambda index: reduce_copy(slot * N, index).wait_recv())
        total = part_in[0, :, at]
        for index in range(1, N):
            total = total + part_in[index, :, at]
        mid[:, at] = total
        for d in order:
            exchange_copy(d, count).start()
        mid_in[pl.ds(me, 1), :, at] = total[None]

    start(1, vis_send, vis_got, *late)

    mean_grad = spread(by_token(mean_grad) / features)
    mean_proj = spread(by_token(mean_proj) / features)
    for first, width in z.cuts:
        grad = inverse * (ups[:, first:first + width] - mean_grad - norm[:, first:first + width] * mean_proj)
        grad_ref[:, first:first + width] = dot(back_ref[...], grad.astype(BF16)).astype(BF16)

    @holding
    def _(count):
        at = slice(0, count * LANES)
        for d in order:
            exchange_copy(d, count).wait()
        total = mid_in[0, :, at]
        for index in range(1, G):
            total = total + mid_in[index, :, at]
        mid[:, at] = total * factor
        others(N, lambda index: gather_copy(index, rep, count).start())
        fin[pl.ds(rep, 1), :, at] = (total * factor)[None]

    slot_code = lax.broadcasted_iota(jnp.int32, (z.padded_slots, 1), 0) * QUADS
    code = jnp.concatenate([slot_code + quad for quad in range(QUADS)], axis=0)
    arrived(1, vis_send, vis_got, PIECES)
    for piece in early + late:
        first, width = z.cuts[piece]
        if piece == late[-1]:
            others(min(N, z.tiles), lambda index: gather_copy(0, index, held(index)).wait_recv())
            for quad in range(QUADS):
                for tile in range(z.tiles):
                    index, at = tile % N, tile // N * LANES
                    row = quad * z.tiles + tile
                    gain_out[row:row + 1, :] = fin[index, quad:quad + 1, at:at + LANES]
                    bias_out[row:row + 1, :] = fin[index, QUADS + quad:QUADS + quad + 1, at:at + LANES]
        arrived(1, vis_send, vis_got, piece)
        block = gather_block(vis_got, onehot(code == row_ref[piece:piece + 1, :]), first, width).astype(BF16)
        for quad in range(QUADS):
            at = quad * z.padded_slots
            visual[:, quad * C + first:quad * C + first + width] = block[at:at + z.slots]
    for tile in range(z.tiles):
        @pl.when(rep != tile % N)
        def _():
            reduce_copy(tile, rep).wait_send()

    @holding
    def _(count):
        others(N, lambda index: gather_copy(index, rep, count).wait_send())

    for piece in pieces:
        for d in order:
            peer = exclusive(me, d, G)
            remote(0, cot_send, cot_got, piece, peer, me).wait_send()
            remote(1, vis_send, vis_got, piece, peer, me).wait_send()


def place_kernel(*refs):
    count = (len(refs) - 1) // 2
    moves = [pltpu.make_async_copy(refs[n], refs[count + n], refs[-1].at[n]) for n in range(count)]
    for move in moves:
        move.start()
    for move in moves:
        move.wait()


def body(encoder_out, destination, norm_gain, norm_bias, cotangent):
    groups, reps = lax.axis_size("enc"), lax.axis_size("rep")
    z = Sizes(encoder_out.shape, cotangent.shape, groups, reps)
    factor = 1.0 / math.sqrt(z.tokens * groups * reps)
    codes = z.codes()
    permutation = z.permutation()
    features = QUADS * z.channels
    rest_rows = max(z.rest_rows, 16)
    block_a, block_b = (groups, max(z.whole, 16), z.channels), (groups, rest_rows, z.width)
    vmem = pl.BlockSpec(memory_space=pltpu.VMEM)
    dma = pltpu.SemaphoreType.DMA
    share = (QUADS * 2, z.share)
    anywhere = pl.BlockSpec(memory_space=pl.ANY)
    rows = features // LANES
    table = jnp.asarray(codes)
    small = [
        pltpu.VMEM((1, z.tokens), jnp.int32),
        pltpu.VMEM((rows, LANES), F32),
        pltpu.VMEM((rows, LANES), F32),
        pltpu.VMEM(permutation.shape, BF16),
        pltpu.VMEM(permutation.shape, BF16),
        pltpu.VMEM(codes.T.shape, jnp.int32),
        pltpu.VMEM(codes.shape, jnp.int32),
    ]
    results = pl.pallas_call(
        functools.partial(kernel, z, factor),
        out_shape=(
            pltpu.VMEM((z.slots, features), BF16),
            pltpu.VMEM((z.patches, z.channels), BF16),
            pltpu.VMEM((rows, LANES), F32),
            pltpu.VMEM((rows, LANES), F32),
        ),
        in_specs=[anywhere] * 9,
        out_specs=(vmem,) * 4,
        scratch_shapes=small + [
            pltpu.VMEM((z.patches, z.channels), BF16),
            pltpu.VMEM((z.slots, features), BF16),
        ]
        + [pltpu.VMEM(shape, BF16) for shape in (block_a, block_b) * 4]
        + [
            pltpu.VMEM((z.patches, z.channels), F32),
            pltpu.VMEM((z.patches, z.channels), F32),
            pltpu.VMEM((QUADS * 2, z.channels), F32),
            pltpu.VMEM((reps,) + share, F32),
            pltpu.VMEM(share, F32),
            pltpu.VMEM((groups,) + share, F32),
            pltpu.VMEM((reps,) + share, F32),
            pltpu.SemaphoreType.REGULAR((groups,)),
            pltpu.SemaphoreType.REGULAR,
            dma((len(small),)),
            dma((2, QUADS)),
            dma,
            dma((2, PIECES + 1, groups)),
            dma((2, PIECES + 1, groups)),
            dma((2, PIECES + 1)),
            dma((z.tiles,)),
            dma((-(-z.tiles // reps), reps)),
            dma((groups,)),
            dma((groups,)),
            dma((reps,)),
            dma((reps,)),
        ],
        compiler_params=pltpu.CompilerParams(collective_id=0, has_side_effects=True, vmem_limit_bytes=60 * 1024 * 1024),
        name="dispatch",
    )(
        encoder_out.reshape(z.patches, z.channels),
        destination.reshape(1, z.tokens),
        norm_gain.reshape(rows, LANES),
        norm_bias.reshape(rows, LANES),
        cotangent,
        jnp.asarray(permutation, BF16),
        jnp.asarray(permutation.T, BF16),
        jnp.asarray(np.ascontiguousarray(codes.T)),
        table,
    )
    visual, grad, gain_sum, bias_sum = pl.pallas_call(
        place_kernel,
        out_shape=tuple(jax.ShapeDtypeStruct(result.shape, result.dtype) for result in results),
        in_specs=[vmem] * 4,
        out_specs=(anywhere,) * 4,
        scratch_shapes=[dma((4,))],
        compiler_params=pltpu.CompilerParams(vmem_limit_bytes=16 * 1024 * 1024),
        name="place",
    )(*results)
    return (visual, grad.reshape(encoder_out.shape), gain_sum.reshape(features), bias_sum.reshape(features))


def solution(mesh):
    placed = (
        P(("enc", "rep"), None, None),
        P(("enc", "rep"), None),
        P(),
        P(),
        P(("enc", "rep"), None),
    )
    return jax.shard_map(
        body,
        mesh=mesh,
        in_specs=placed,
        out_specs=(P(("enc", "rep"), None), P(("enc", "rep"), None, None), P(), P()),
        check_vma=False,
    )
```

```python
import functools
import math

import jax
import jax.numpy as jnp
import numpy as np
from jax import lax
from jax.experimental import pallas as pl
from jax.experimental.pallas import tpu as pltpu
from jax.sharding import PartitionSpec as P

epsilon = 1e-05
LANES = 128
QUADS = 4
PIECES = 4
F32 = jnp.float32
BF16 = jnp.bfloat16


def onehot(mask):
    return jnp.where(mask, 1.0, 0.0).astype(BF16)


def dot(a, b):
    return jnp.dot(a, b, preferred_element_type=F32)


class Sizes:
    def __init__(self, encoder_shape, slot_shape, groups, reps):
        height, across, self.channels = encoder_shape
        self.height, self.across = height, across
        self.groups, self.reps = groups, reps
        self.patches = height * across
        self.tokens = self.patches // QUADS
        self.slots = slot_shape[0]
        self.capacity = self.slots // groups
        folded = self.capacity * QUADS
        self.whole = folded // 16 * 16
        self.rest = folded - self.whole
        self.rest_rows = self.rest * PIECES
        self.rows_a = groups * self.whole
        self.rows_b = groups * self.rest_rows
        tiles = self.channels // LANES
        self.width = -(-tiles // PIECES) * LANES
        self.cuts = []
        start, width = 0, self.channels - (-(-self.channels // self.width) - 1) * self.width
        while start < self.channels:
            self.cuts.append((start, width))
            start, width = start + width, self.width
        self.tiles = tiles
        self.base, self.extra = divmod(tiles, reps)
        self.share = -(-tiles // reps) * LANES
        self.padded_slots = -(-self.slots // 16) * 16

    def codes(self):
        out = np.full((PIECES, self.rows_a + self.rows_b), -1, np.int32)
        for group in range(self.groups):
            for row in range(self.whole):
                out[:, group * self.whole + row] = group * self.capacity * QUADS + row
            for row in range(self.rest):
                for piece in range(PIECES):
                    at = self.rows_a + group * self.rest_rows + row * PIECES + piece
                    out[piece, at] = group * self.capacity * QUADS + self.whole + row
        return out

    def permutation(self):
        out = np.zeros((self.patches, self.patches), np.float32)
        half = self.across // 2
        for token in range(self.tokens):
            a, b = divmod(token, half)
            for quad in range(QUADS):
                dy, dx = divmod(quad, 2)
                out[quad * self.tokens + token, (2 * a + dy) * self.across + 2 * b + dx] = 1.0
        return out


def take(z, buffers, pick, first, width, ready):
    a, b = buffers
    block = None
    if z.rows_b:
        block = dot(pick[:, z.rows_a:], b[...].reshape(z.rows_b, z.width)[:, :width])
    ready()
    if z.rows_a:
        term = dot(pick[:, :z.rows_a], a[:, :, first:first + width].reshape(z.rows_a, width))
        block = term if block is None else block + term
    return block


def exclusive(me, d, count):
    if count & (count - 1):
        return lax.rem(me + d, count)
    bit = 1
    while bit < count:
        if d & bit:
            me = me + bit - 2 * bit * lax.rem(me // bit, 2)
        bit *= 2
    return me


def nearest(me, k):
    return jnp.where(k < me, me - 1 - k, k + 1)


def kernel(z, factor, x_hbm, own_hbm, gain_hbm, bias_hbm, cot_hbm, perm_hbm, back_hbm, col_hbm, row_hbm,
           visual, grad_ref, gain_out, bias_out,
           own_ref, gain_ref, bias_ref, perm_ref, back_ref, col_ref, row_ref, x_ref, cot_ref, cs_a, cs_b, cr_a, cr_b, vs_a, vs_b, vr_a, vr_b, norm, ups, part, part_in, mid, mid_in, fin,
           here_enc, here_rep, in_sem, cot_sem, x_sem, send_sem, recv_sem, self_sem, rs_send, rs_recv, ex_send, ex_recv, ag_send, ag_recv):
    G, N, T = z.groups, z.reps, z.tokens
    C, rows_a, rows_b = z.channels, z.rows_a, z.rows_b
    me, rep = lax.axis_index("enc"), lax.axis_index("rep")
    order = list(range(1, G))
    features = QUADS * C

    barrier = pltpu.get_barrier_semaphore()

    def twin(index):
        return index + 1 - 2 * lax.rem(index, 2) if N % 2 == 0 else index

    def greet(semaphore, axis, count, at, later):
        for place in range(1, count) if later else range(count - 2, -1, -1):
            @pl.when(place > at if later else place < at)
            def _():
                index = twin(place) if axis == "rep" else place
                pl.semaphore_signal(semaphore, inc=1, device_id={axis: index}, device_id_type=pl.DeviceIdType.MESH)

    rank = twin(rep)
    parted = [z.cuts[0], (z.cuts[0][1], C - z.cuts[0][1])] if len(z.cuts) > 1 else [z.cuts[0]]

    def cot_copy(half, quad):
        first, width = parted[half]
        at = pl.ds(quad * C + first, width)
        return pltpu.make_async_copy(cot_hbm.at[:, at], cot_ref.at[:, at], cot_sem.at[half, quad])

    small = [
        pltpu.make_async_copy(source, target, in_sem.at[n])
        for n, (source, target) in enumerate((
            (col_hbm, col_ref), (perm_hbm, perm_ref), (own_hbm, own_ref), (gain_hbm, gain_ref),
            (bias_hbm, bias_ref), (row_hbm, row_ref), (back_hbm, back_ref)))
    ]
    x_copy = pltpu.make_async_copy(x_hbm, x_ref, x_sem)
    small[0].start()
    for quad in range(QUADS):
        cot_copy(0, quad).start()
    greet(barrier, "enc", G, me, True)
    greet(barrier, "rep", N, rank, True)

    @pl.when(me + rank > 0)
    def _():
        pl.semaphore_wait(barrier, me + rank)

    greet(here_enc.at[me], "enc", G, me, False)
    for quad in range(QUADS):
        for half in range(1, len(parted)):
            cot_copy(half, quad).start()

    def views(which, buffers, index, piece):
        a, b = buffers
        if piece == PIECES:
            return b.at[index]
        start, width = z.cuts[piece]
        if which and piece in joined:
            width = sum(z.cuts[n][1] for n in joined)
        return a.at[index, :, pl.ds(start, width)]

    def remote(which, source, target, piece, peer, sender):
        return pltpu.make_async_remote_copy(
            src_ref=views(which, source, peer, piece), dst_ref=views(which, target, sender, piece),
            send_sem=send_sem.at[which, piece, peer], recv_sem=recv_sem.at[which, piece, sender],
            device_id={"enc": peer}, device_id_type=pl.DeviceIdType.MESH)

    def own(which, source, target, piece):
        return pltpu.make_async_copy(views(which, source, me, piece), views(which, target, me, piece), self_sem.at[which, piece])

    count = len(z.cuts)
    joined = list(range(1, count - 1))
    everything = (list(range(count)) if rows_a else []) + ([PIECES] if rows_b else [])
    pieces = (everything, [piece for piece in everything if piece not in joined[1:]])

    def start(which, source, target, *chosen):
        chosen = [piece for piece in chosen if piece in pieces[which]]
        for d in order:
            for piece in chosen:
                remote(which, source, target, piece, exclusive(me, d, G), me).start()
        for piece in chosen:
            own(which, source, target, piece).start()

    def start_first(piece, near):
        if piece not in pieces[0]:
            return
        for k in range(min(2, G - 1)) if near else range(2, G - 1):
            peer = nearest(me, k)

            @pl.when(peer > me)
            def _():
                pl.semaphore_wait(here_enc.at[peer], 1)

            remote(0, cot_send, cot_got, piece, peer, me).start()
        if near:
            own(0, cot_send, cot_got, piece).start()

    def arrived(which, source, target, piece):
        if piece not in pieces[which]:
            return
        for d in order:
            peer = exclusive(me, d, G)
            remote(which, source, target, piece, peer, peer).wait_recv()
        own(which, source, target, piece).wait()

    def store_block(buffers, piece, value, rest):
        a, b = buffers
        first, width = z.cuts[piece]
        if rows_a:
            a[:, :, first:first + width] = value[:rows_a].astype(BF16).reshape(G, z.whole, width)
        if rows_b:
            more = value[rows_a:]
            if width < z.width:
                more = jnp.concatenate([more, jnp.zeros((rows_b, z.width - width), F32)], axis=1)
            return more if rest is None else rest + more
        return None

    gather_block = functools.partial(take, z)

    cot_send, cot_got, vis_send, vis_got = (cs_a, cs_b), (cr_a, cr_b), (vs_a, vs_b), (vr_a, vr_b)

    rest = None
    ahead = min(2, count)
    lead = 0 if rows_a else PIECES
    small[0].wait()
    slot_lane = lax.broadcasted_iota(jnp.int32, (rows_a + rows_b, z.slots), 1) * QUADS
    for piece, (first, width) in enumerate(z.cuts):
        block = None
        picks = [onehot(col_ref[:, piece:piece + 1] == slot_lane + quad) for quad in range(QUADS)]
        for quad in range(QUADS):
            if piece < 2:
                cot_copy(piece, quad).wait()
            term = dot(picks[quad], cot_ref[:, quad * C + first:quad * C + first + width])
            block = term if block is None else block + term
        rest = store_block(cot_send, piece, block, rest)
        if piece == lead:
            start_first(lead, True)
        if piece == ahead - 1 and lead == 0:
            start_first(lead, False)
        if 0 < piece < ahead:
            start(0, cot_send, cot_got, piece)
        if piece == 0:
            greet(here_rep, "rep", N, rank, False)
            x_copy.start()
            for copy in small[1:]:
                copy.start()
    if rows_b:
        cs_b[...] = rest.astype(BF16).reshape(G, z.rest_rows, z.width)
        if lead == PIECES:
            start_first(lead, True)
            start_first(lead, False)
        else:
            start(0, cot_send, cot_got, PIECES)
    for piece in range(ahead, count):
        start(0, cot_send, cot_got, piece)

    for copy in small[1:]:
        copy.wait()
    lane = lax.broadcasted_iota(jnp.int32, (T, QUADS * T), 1)
    token = lax.broadcasted_iota(jnp.int32, (T, QUADS * T), 0)
    quad_of = sum((lane >= n * T).astype(jnp.int32) for n in range(1, QUADS))
    token_of = lane - quad_of * T
    corner = lax.broadcasted_iota(jnp.int32, (T, T), 0) == lax.broadcasted_iota(jnp.int32, (T, T), 1)
    owner = jnp.sum(jnp.where(corner, own_ref[...].astype(F32), 0.0), axis=1, keepdims=True)
    owner_row = jnp.sum(jnp.where(token == token_of, owner, 0.0), axis=0, keepdims=True)
    rank_row = jnp.sum(jnp.where((owner == owner_row) & (token < token_of), 1.0, 0.0), axis=0, keepdims=True)
    code_row = (owner_row * z.capacity + rank_row) * QUADS + quad_of[:1].astype(F32)
    square = (QUADS * T, QUADS * T)
    eye = lax.broadcasted_iota(jnp.int32, square, 0) == lax.broadcasted_iota(jnp.int32, square, 1)
    code_col = jnp.sum(jnp.where(eye, code_row, 0.0), axis=1, keepdims=True)

    def by_token(column):
        total = column[:T]
        for quad in range(1, QUADS):
            total = total + column[quad * T:(quad + 1) * T]
        return total

    def spread(column):
        return jnp.concatenate([column] * QUADS, axis=0)

    def params(ref, first, width):
        def row(at):
            return jnp.concatenate([ref[n:n + 1, :] for n in range(at // LANES, (at + width) // LANES)], axis=1)

        return jnp.concatenate([jnp.broadcast_to(row(quad * C + first), (T, width)) for quad in range(QUADS)], axis=0)

    x_copy.wait()

    total = jnp.zeros((QUADS * T, 1), F32)
    for first, width in z.cuts:
        values = dot(perm_ref[...], x_ref[:, first:first + width])
        norm[:, first:first + width] = values
        total = total + jnp.sum(values, axis=1, keepdims=True)
    center = spread(by_token(total) / features)
    total = jnp.zeros((QUADS * T, 1), F32)
    for first, width in z.cuts:
        values = norm[:, first:first + width] - center
        total = total + jnp.sum(values * values, axis=1, keepdims=True)
    inverse = spread(lax.rsqrt(by_token(total) / features + epsilon))

    rest = None
    for piece, (first, width) in enumerate(z.cuts):
        values = (norm[:, first:first + width] - center) * inverse
        norm[:, first:first + width] = values
        output = values * params(gain_ref, first, width) + params(bias_ref, first, width)
        pick = onehot(col_ref[:, piece:piece + 1].astype(F32) == code_row)
        rest = store_block(vis_send, piece, dot(pick, output.astype(BF16)), rest)
    if rows_b:
        vs_b[...] = rest.astype(BF16).reshape(G, z.rest_rows, z.width)
    early, late = list(range(1, count - 1)), [count - 1, 0][-count:]
    start(1, vis_send, vis_got, PIECES)
    for piece in early:
        start(1, vis_send, vis_got, piece)

    def lanes(tile):
        return pl.ds(tile * LANES, LANES)

    def reduce_copy(tile, sender):
        slot, index = divmod(tile, N)
        return pltpu.make_async_remote_copy(
            src_ref=part.at[:, lanes(tile)], dst_ref=part_in.at[sender, :, lanes(slot)],
            send_sem=rs_send.at[tile], recv_sem=rs_recv.at[slot, sender],
            device_id={"rep": index}, device_id_type=pl.DeviceIdType.MESH)

    def held(index):
        return z.base + (index < z.extra)

    def holding(act):
        if z.extra:
            @pl.when(rep < z.extra)
            def _():
                act(z.base + 1)

        if z.base:
            @pl.when(rep >= z.extra)
            def _():
                act(z.base)

    def exchange_copy(d, count):
        peer = exclusive(me, d, G)
        at = pl.ds(0, count * LANES)
        return pltpu.make_async_remote_copy(
            src_ref=mid.at[:, at], dst_ref=mid_in.at[me, :, at], send_sem=ex_send.at[d], recv_sem=ex_recv.at[d],
            device_id={"enc": peer}, device_id_type=pl.DeviceIdType.MESH)

    def gather_copy(peer, sender, count):
        at = pl.ds(0, count * LANES)
        return pltpu.make_async_remote_copy(
            src_ref=mid.at[:, at], dst_ref=fin.at[sender, :, at], send_sem=ag_send.at[peer], recv_sem=ag_recv.at[sender],
            device_id={"rep": peer}, device_id_type=pl.DeviceIdType.MESH)

    def others(count, act):
        for index in range(count):
            @pl.when(rep != index)
            def _():
                act(index)

    mean_grad = jnp.zeros((QUADS * T, 1), F32)
    mean_proj = jnp.zeros((QUADS * T, 1), F32)
    arrived(0, cot_send, cot_got, PIECES)
    sent = 0
    for piece, (first, width) in enumerate(z.cuts):
        pick = onehot(code_col == row_ref[piece:piece + 1, :].astype(F32))
        upstream = gather_block(cot_got, pick, first, width, functools.partial(arrived, 0, cot_send, cot_got, piece))
        normed = norm[:, first:first + width]
        product = upstream * normed
        scale = params(gain_ref, first, width)
        scaled = upstream * scale
        ups[:, first:first + width] = scaled
        mean_grad = mean_grad + jnp.sum(scaled, axis=1, keepdims=True)
        mean_proj = mean_proj + jnp.sum(scaled * normed, axis=1, keepdims=True)
        part[:, first:first + width] = jnp.concatenate(
            [jnp.sum(value[quad * T:(quad + 1) * T], axis=0, keepdims=True)
             for value in (product, upstream) for quad in range(QUADS)], axis=0)
        done = (first + width) // LANES
        if sent == 0:
            @pl.when(rank < N - 1)
            def _():
                pl.semaphore_wait(here_rep, N - 1 - rank)
        for tile in range(sent, done):
            slot, index = divmod(tile, N)

            @pl.when(rep != index)
            def _():
                reduce_copy(tile, rep).start()

            @pl.when(rep == index)
            def _():
                part_in[index, :, slot * LANES:(slot + 1) * LANES] = part[:, tile * LANES:(tile + 1) * LANES]
        sent = done

    @holding
    def _(count):
        at = slice(0, count * LANES)
        for slot in range(count):
            others(N, lambda index: reduce_copy(slot * N, index).wait_recv())
        total = part_in[0, :, at]
        for index in range(1, N):
            total = total + part_in[index, :, at]
        mid[:, at] = total
        for d in order[::-1]:
            exchange_copy(d, count).start()
        mid_in[pl.ds(me, 1), :, at] = total[None]

    start(1, vis_send, vis_got, *late)

    mean_grad = spread(by_token(mean_grad) / features)
    mean_proj = spread(by_token(mean_proj) / features)
    for first, width in z.cuts:
        grad = inverse * (ups[:, first:first + width] - mean_grad - norm[:, first:first + width] * mean_proj)
        grad_ref[:, first:first + width] = dot(back_ref[...], grad.astype(BF16)).astype(BF16)

    @holding
    def _(count):
        at = slice(0, count * LANES)
        for d in order:
            exchange_copy(d, count).wait()
        total = mid_in[0, :, at]
        for index in range(1, G):
            total = total + mid_in[index, :, at]
        mid[:, at] = total * factor
        others(N, lambda index: gather_copy(index, rep, count).start())
        fin[pl.ds(rep, 1), :, at] = (total * factor)[None]

    def sends_done(which, source, target, chosen):
        for piece in chosen:
            if piece in pieces[which]:
                for d in order:
                    remote(which, source, target, piece, exclusive(me, d, G), me).wait_send()

    def settle():
        for tile in range(z.tiles):
            @pl.when(rep != tile % N)
            def _():
                reduce_copy(tile, rep).wait_send()

        @holding
        def _(count):
            others(N, lambda index: gather_copy(index, rep, count).wait_send())

        sends_done(0, cot_send, cot_got, list(range(count)) + [PIECES])
        sends_done(1, vis_send, vis_got, early + [PIECES])

    slot_code = lax.broadcasted_iota(jnp.int32, (z.padded_slots, 1), 0) * QUADS
    code = jnp.concatenate([slot_code + quad for quad in range(QUADS)], axis=0)
    arrived(1, vis_send, vis_got, PIECES)
    for piece in early + late:
        first, width = z.cuts[piece]
        if piece == late[-1]:
            others(min(N, z.tiles), lambda index: gather_copy(0, index, held(index)).wait_recv())
            for quad in range(QUADS):
                for tile in range(z.tiles):
                    index, at = tile % N, tile // N * LANES
                    row = quad * z.tiles + tile
                    gain_out[row:row + 1, :] = fin[index, quad:quad + 1, at:at + LANES]
                    bias_out[row:row + 1, :] = fin[index, QUADS + quad:QUADS + quad + 1, at:at + LANES]
            settle()
        pick = onehot(code == row_ref[piece:piece + 1, :])
        block = gather_block(
            vis_got, pick, first, width, functools.partial(arrived, 1, vis_send, vis_got, piece)).astype(BF16)
        for quad in range(QUADS):
            at = quad * z.padded_slots
            visual[:, quad * C + first:quad * C + first + width] = block[at:at + z.slots]
    sends_done(1, vis_send, vis_got, late)


def place_kernel(*refs):
    count = (len(refs) - 1) // 2
    moves = [pltpu.make_async_copy(refs[n], refs[count + n], refs[-1].at[n]) for n in range(count)]
    for move in moves:
        move.start()
    for move in moves:
        move.wait()


def body(encoder_out, destination, norm_gain, norm_bias, cotangent):
    groups, reps = lax.axis_size("enc"), lax.axis_size("rep")
    z = Sizes(encoder_out.shape, cotangent.shape, groups, reps)
    factor = 1.0 / math.sqrt(z.tokens * groups * reps)
    codes = z.codes()
    permutation = z.permutation()
    features = QUADS * z.channels
    rest_rows = max(z.rest_rows, 16)
    block_a, block_b = (groups, max(z.whole, 16), z.channels), (groups, rest_rows, z.width)
    vmem = pl.BlockSpec(memory_space=pltpu.VMEM)
    dma = pltpu.SemaphoreType.DMA
    share = (QUADS * 2, z.share)
    anywhere = pl.BlockSpec(memory_space=pl.ANY)
    rows = features // LANES
    table = jnp.asarray(codes)
    small = [
        pltpu.VMEM((1, z.tokens), jnp.int32),
        pltpu.VMEM((rows, LANES), F32),
        pltpu.VMEM((rows, LANES), F32),
        pltpu.VMEM(permutation.shape, BF16),
        pltpu.VMEM(permutation.shape, BF16),
        pltpu.VMEM(codes.T.shape, jnp.int32),
        pltpu.VMEM(codes.shape, jnp.int32),
    ]
    results = pl.pallas_call(
        functools.partial(kernel, z, factor),
        out_shape=(
            pltpu.VMEM((z.slots, features), BF16),
            pltpu.VMEM((z.patches, z.channels), BF16),
            pltpu.VMEM((rows, LANES), F32),
            pltpu.VMEM((rows, LANES), F32),
        ),
        in_specs=[anywhere] * 9,
        out_specs=(vmem,) * 4,
        scratch_shapes=small + [
            pltpu.VMEM((z.patches, z.channels), BF16),
            pltpu.VMEM((z.slots, features), BF16),
        ]
        + [pltpu.VMEM(shape, BF16) for shape in (block_a, block_b) * 4]
        + [
            pltpu.VMEM((z.patches, z.channels), F32),
            pltpu.VMEM((z.patches, z.channels), F32),
            pltpu.VMEM((QUADS * 2, z.channels), F32),
            pltpu.VMEM((reps,) + share, F32),
            pltpu.VMEM(share, F32),
            pltpu.VMEM((groups,) + share, F32),
            pltpu.VMEM((reps,) + share, F32),
            pltpu.SemaphoreType.REGULAR((groups,)),
            pltpu.SemaphoreType.REGULAR,
            dma((len(small),)),
            dma((2, QUADS)),
            dma,
            dma((2, PIECES + 1, groups)),
            dma((2, PIECES + 1, groups)),
            dma((2, PIECES + 1)),
            dma((z.tiles,)),
            dma((-(-z.tiles // reps), reps)),
            dma((groups,)),
            dma((groups,)),
            dma((reps,)),
            dma((reps,)),
        ],
        compiler_params=pltpu.CompilerParams(collective_id=0, has_side_effects=True, vmem_limit_bytes=60 * 1024 * 1024),
        name="dispatch",
    )(
        encoder_out.reshape(z.patches, z.channels),
        destination.reshape(1, z.tokens),
        norm_gain.reshape(rows, LANES),
        norm_bias.reshape(rows, LANES),
        cotangent,
        jnp.asarray(permutation, BF16),
        jnp.asarray(permutation.T, BF16),
        jnp.asarray(np.ascontiguousarray(codes.T)),
        table,
    )
    visual, grad, gain_sum, bias_sum = pl.pallas_call(
        place_kernel,
        out_shape=tuple(jax.ShapeDtypeStruct(result.shape, result.dtype) for result in results),
        in_specs=[vmem] * 4,
        out_specs=(anywhere,) * 4,
        scratch_shapes=[dma((4,))],
        compiler_params=pltpu.CompilerParams(vmem_limit_bytes=16 * 1024 * 1024),
        name="place",
    )(*results)
    return (visual, grad.reshape(encoder_out.shape), gain_sum.reshape(features), bias_sum.reshape(features))


def solution(mesh):
    placed = (
        P(("enc", "rep"), None, None),
        P(("enc", "rep"), None),
        P(),
        P(),
        P(("enc", "rep"), None),
    )
    return jax.shard_map(
        body,
        mesh=mesh,
        in_specs=placed,
        out_specs=(P(("enc", "rep"), None), P(("enc", "rep"), None, None), P(), P()),
        check_vma=False,
    )
```

```python
import functools
import math

import jax
import jax.numpy as jnp
import numpy as np
from jax import lax
from jax.experimental import pallas as pl
from jax.experimental.pallas import tpu as pltpu
from jax.sharding import PartitionSpec as P

epsilon = 1e-05
LANES = 128
QUADS = 4
PIECES = 4
F32 = jnp.float32
BF16 = jnp.bfloat16


def onehot(mask):
    return jnp.where(mask, 1.0, 0.0).astype(BF16)


def dot(a, b):
    return jnp.dot(a, b, preferred_element_type=F32)


class Sizes:
    def __init__(self, encoder_shape, slot_shape, groups, reps):
        height, across, self.channels = encoder_shape
        self.height, self.across = height, across
        self.groups, self.reps = groups, reps
        self.patches = height * across
        self.tokens = self.patches // QUADS
        self.slots = slot_shape[0]
        self.capacity = self.slots // groups
        folded = self.capacity * QUADS
        self.whole = folded // 16 * 16
        self.rest = folded - self.whole
        self.rest_rows = self.rest * PIECES
        self.rows_a = groups * self.whole
        self.rows_b = groups * self.rest_rows
        tiles = self.channels // LANES
        self.width = -(-tiles // PIECES) * LANES
        self.cuts = []
        start, width = 0, self.channels - (-(-self.channels // self.width) - 1) * self.width
        while start < self.channels:
            self.cuts.append((start, width))
            start, width = start + width, self.width
        self.tiles = tiles
        self.base, self.extra = divmod(tiles, reps)
        self.share = -(-tiles // reps) * LANES
        self.padded_slots = -(-self.slots // 16) * 16

    def codes(self):
        out = np.full((PIECES, self.rows_a + self.rows_b), -1, np.int32)
        for group in range(self.groups):
            for row in range(self.whole):
                out[:, group * self.whole + row] = group * self.capacity * QUADS + row
            for row in range(self.rest):
                for piece in range(PIECES):
                    at = self.rows_a + group * self.rest_rows + row * PIECES + piece
                    out[piece, at] = group * self.capacity * QUADS + self.whole + row
        return out

    def permutation(self):
        out = np.zeros((self.patches, self.patches), np.float32)
        half = self.across // 2
        for token in range(self.tokens):
            a, b = divmod(token, half)
            for quad in range(QUADS):
                dy, dx = divmod(quad, 2)
                out[quad * self.tokens + token, (2 * a + dy) * self.across + 2 * b + dx] = 1.0
        return out


def take(z, buffers, pick, first, width, ready):
    a, b = buffers
    block = None
    if z.rows_b:
        block = dot(pick[:, z.rows_a:], b[...].reshape(z.rows_b, z.width)[:, :width])
    ready()
    if z.rows_a:
        term = dot(pick[:, :z.rows_a], a[:, :, first:first + width].reshape(z.rows_a, width))
        block = term if block is None else block + term
    return block


def exclusive(me, d, count):
    if count & (count - 1):
        return lax.rem(me + d, count)
    bit = 1
    while bit < count:
        if d & bit:
            me = me + bit - 2 * bit * lax.rem(me // bit, 2)
        bit *= 2
    return me


def nearest(me, k):
    return jnp.where(k < me, me - 1 - k, k + 1)


def kernel(z, factor, x_hbm, own_hbm, gain_hbm, bias_hbm, cot_hbm, perm_hbm, back_hbm, col_hbm, row_hbm,
           visual, grad_ref, gain_out, bias_out,
           own_ref, gain_ref, bias_ref, perm_ref, back_ref, col_ref, row_ref, x_ref, cot_ref, cs_a, cs_b, cr_a, cr_b, vs_a, vs_b, vr_a, vr_b, norm, ups, part, part_in, mid, mid_in, fin,
           here_enc, here_rep, in_sem, cot_sem, x_sem, send_sem, recv_sem, self_sem, rs_send, rs_recv, ex_send, ex_recv, ag_send, ag_recv):
    G, N, T = z.groups, z.reps, z.tokens
    C, rows_a, rows_b = z.channels, z.rows_a, z.rows_b
    me, rep = lax.axis_index("enc"), lax.axis_index("rep")
    order = list(range(1, G))
    features = QUADS * C

    barrier = pltpu.get_barrier_semaphore()

    def twin(index):
        return index + 1 - 2 * lax.rem(index, 2) if N % 2 == 0 else index

    def greet(semaphore, axis, count, at, later):
        for place in range(1, count) if later else range(count - 2, -1, -1):
            @pl.when(place > at if later else place < at)
            def _():
                index = twin(place) if axis == "rep" else place
                pl.semaphore_signal(semaphore, inc=1, device_id={axis: index}, device_id_type=pl.DeviceIdType.MESH)

    rank = twin(rep)
    parted = [z.cuts[0], (z.cuts[0][1], C - z.cuts[0][1])] if len(z.cuts) > 1 else [z.cuts[0]]

    def cot_copy(half, quad):
        first, width = parted[half]
        at = pl.ds(quad * C + first, width)
        return pltpu.make_async_copy(cot_hbm.at[:, at], cot_ref.at[:, at], cot_sem.at[half, quad])

    small = [
        pltpu.make_async_copy(source, target, in_sem.at[n])
        for n, (source, target) in enumerate((
            (col_hbm, col_ref), (perm_hbm, perm_ref), (own_hbm, own_ref), (gain_hbm, gain_ref),
            (bias_hbm, bias_ref), (row_hbm, row_ref), (back_hbm, back_ref)))
    ]
    x_copy = pltpu.make_async_copy(x_hbm, x_ref, x_sem)
    small[0].start()
    for quad in range(QUADS):
        cot_copy(0, quad).start()
    greet(barrier, "enc", G, me, True)
    greet(barrier, "rep", N, rank, True)

    @pl.when(me + rank > 0)
    def _():
        pl.semaphore_wait(barrier, me + rank)

    greet(here_enc.at[me], "enc", G, me, False)
    for quad in range(QUADS):
        for half in range(1, len(parted)):
            cot_copy(half, quad).start()

    def views(which, buffers, index, piece):
        a, b = buffers
        if piece == PIECES:
            return b.at[index]
        start, width = z.cuts[piece]
        if which and piece in joined:
            width = sum(z.cuts[n][1] for n in joined)
        return a.at[index, :, pl.ds(start, width)]

    def remote(which, source, target, piece, peer, sender):
        return pltpu.make_async_remote_copy(
            src_ref=views(which, source, peer, piece), dst_ref=views(which, target, sender, piece),
            send_sem=send_sem.at[which, piece, peer], recv_sem=recv_sem.at[which, piece, sender],
            device_id={"enc": peer}, device_id_type=pl.DeviceIdType.MESH)

    def own(which, source, target, piece):
        return pltpu.make_async_copy(views(which, source, me, piece), views(which, target, me, piece), self_sem.at[which, piece])

    count = len(z.cuts)
    joined = list(range(1, count - 1))
    everything = (list(range(count)) if rows_a else []) + ([PIECES] if rows_b else [])
    pieces = (everything, [piece for piece in everything if piece not in joined[1:]])

    def start(which, source, target, *chosen):
        chosen = [piece for piece in chosen if piece in pieces[which]]
        for d in order:
            for piece in chosen:
                remote(which, source, target, piece, exclusive(me, d, G), me).start()
        for piece in chosen:
            own(which, source, target, piece).start()

    def start_first(piece, near):
        if piece not in pieces[0]:
            return
        for k in range(min(2, G - 1)) if near else range(2, G - 1):
            peer = nearest(me, k)

            @pl.when(peer > me)
            def _():
                pl.semaphore_wait(here_enc.at[peer], 1)

            remote(0, cot_send, cot_got, piece, peer, me).start()
        if near:
            own(0, cot_send, cot_got, piece).start()

    def arrived(which, source, target, piece):
        if piece not in pieces[which]:
            return
        for d in order:
            peer = exclusive(me, d, G)
            remote(which, source, target, piece, peer, peer).wait_recv()
        own(which, source, target, piece).wait()

    def store_block(buffers, piece, value, rest):
        a, b = buffers
        first, width = z.cuts[piece]
        if rows_a:
            a[:, :, first:first + width] = value[:rows_a].astype(BF16).reshape(G, z.whole, width)
        if rows_b:
            more = value[rows_a:]
            if width < z.width:
                more = jnp.concatenate([more, jnp.zeros((rows_b, z.width - width), F32)], axis=1)
            return more if rest is None else rest + more
        return None

    gather_block = functools.partial(take, z)

    cot_send, cot_got, vis_send, vis_got = (cs_a, cs_b), (cr_a, cr_b), (vs_a, vs_b), (vr_a, vr_b)

    rest = None
    ahead = min(2, count)
    lead = 0 if rows_a else PIECES
    small[0].wait()
    slot_lane = lax.broadcasted_iota(jnp.int32, (rows_a + rows_b, z.slots), 1) * QUADS
    for piece, (first, width) in enumerate(z.cuts):
        block = None
        picks = [onehot(col_ref[:, piece:piece + 1] == slot_lane + quad) for quad in range(QUADS)]
        for quad in range(QUADS):
            if piece < 2:
                cot_copy(piece, quad).wait()
            term = dot(picks[quad], cot_ref[:, quad * C + first:quad * C + first + width])
            block = term if block is None else block + term
        rest = store_block(cot_send, piece, block, rest)
        if piece == lead:
            start_first(lead, True)
        if piece == ahead - 1 and lead == 0:
            start_first(lead, False)
        if 0 < piece < ahead:
            start(0, cot_send, cot_got, piece)
        if piece == 0:
            greet(here_rep, "rep", N, rank, False)
            x_copy.start()
            for copy in small[1:]:
                copy.start()
    if rows_b:
        cs_b[...] = rest.astype(BF16).reshape(G, z.rest_rows, z.width)
        if lead == PIECES:
            start_first(lead, True)
            start_first(lead, False)
        else:
            start(0, cot_send, cot_got, PIECES)
    for piece in range(ahead, count):
        start(0, cot_send, cot_got, piece)

    for copy in small[1:]:
        copy.wait()
    lane = lax.broadcasted_iota(jnp.int32, (T, QUADS * T), 1)
    token = lax.broadcasted_iota(jnp.int32, (T, QUADS * T), 0)
    quad_of = sum((lane >= n * T).astype(jnp.int32) for n in range(1, QUADS))
    token_of = lane - quad_of * T
    corner = lax.broadcasted_iota(jnp.int32, (T, T), 0) == lax.broadcasted_iota(jnp.int32, (T, T), 1)
    owner = jnp.sum(jnp.where(corner, own_ref[...].astype(F32), 0.0), axis=1, keepdims=True)
    owner_row = jnp.sum(jnp.where(token == token_of, owner, 0.0), axis=0, keepdims=True)
    rank_row = jnp.sum(jnp.where((owner == owner_row) & (token < token_of), 1.0, 0.0), axis=0, keepdims=True)
    code_row = (owner_row * z.capacity + rank_row) * QUADS + quad_of[:1].astype(F32)
    square = (QUADS * T, QUADS * T)
    eye = lax.broadcasted_iota(jnp.int32, square, 0) == lax.broadcasted_iota(jnp.int32, square, 1)
    code_col = jnp.sum(jnp.where(eye, code_row, 0.0), axis=1, keepdims=True)

    def by_token(column):
        total = column[:T]
        for quad in range(1, QUADS):
            total = total + column[quad * T:(quad + 1) * T]
        return total

    def spread(column):
        return jnp.concatenate([column] * QUADS, axis=0)

    def params(ref, first, width):
        def row(at):
            return jnp.concatenate([ref[n:n + 1, :] for n in range(at // LANES, (at + width) // LANES)], axis=1)

        return jnp.concatenate([jnp.broadcast_to(row(quad * C + first), (T, width)) for quad in range(QUADS)], axis=0)

    x_copy.wait()

    total = jnp.zeros((QUADS * T, 1), F32)
    for first, width in z.cuts:
        values = dot(perm_ref[...], x_ref[:, first:first + width])
        norm[:, first:first + width] = values
        total = total + jnp.sum(values, axis=1, keepdims=True)
    center = spread(by_token(total) / features)
    total = jnp.zeros((QUADS * T, 1), F32)
    for first, width in z.cuts:
        values = norm[:, first:first + width] - center
        total = total + jnp.sum(values * values, axis=1, keepdims=True)
    inverse = spread(lax.rsqrt(by_token(total) / features + epsilon))

    rest = None
    for piece, (first, width) in enumerate(z.cuts):
        values = (norm[:, first:first + width] - center) * inverse
        norm[:, first:first + width] = values
        output = values * params(gain_ref, first, width) + params(bias_ref, first, width)
        pick = onehot(col_ref[:, piece:piece + 1].astype(F32) == code_row)
        rest = store_block(vis_send, piece, dot(pick, output.astype(BF16)), rest)
    if rows_b:
        vs_b[...] = rest.astype(BF16).reshape(G, z.rest_rows, z.width)
    early, late = list(range(1, count - 1)), [count - 1, 0][-count:]
    start(1, vis_send, vis_got, PIECES)
    for piece in early:
        start(1, vis_send, vis_got, piece)

    def lanes(tile):
        return pl.ds(tile * LANES, LANES)

    def reduce_copy(tile, sender):
        slot, index = tile // N, (tile - 1) % N
        return pltpu.make_async_remote_copy(
            src_ref=part.at[:, lanes(tile)], dst_ref=part_in.at[sender, :, lanes(slot)],
            send_sem=rs_send.at[tile], recv_sem=rs_recv.at[slot, sender],
            device_id={"rep": index}, device_id_type=pl.DeviceIdType.MESH)

    def held(index):
        return z.base + ((index + 1) % N < z.extra)

    def holding(act):
        if z.extra:
            @pl.when(lax.rem(rep + 1, N) < z.extra)
            def _():
                act(z.base + 1)

        if z.base:
            @pl.when(lax.rem(rep + 1, N) >= z.extra)
            def _():
                act(z.base)

    def exchange_copy(d, count):
        peer = exclusive(me, d, G)
        at = pl.ds(0, count * LANES)
        return pltpu.make_async_remote_copy(
            src_ref=mid.at[:, at], dst_ref=mid_in.at[me, :, at], send_sem=ex_send.at[d], recv_sem=ex_recv.at[d],
            device_id={"enc": peer}, device_id_type=pl.DeviceIdType.MESH)

    def gather_copy(peer, sender, count):
        at = pl.ds(0, count * LANES)
        return pltpu.make_async_remote_copy(
            src_ref=mid.at[:, at], dst_ref=fin.at[sender, :, at], send_sem=ag_send.at[peer], recv_sem=ag_recv.at[sender],
            device_id={"rep": peer}, device_id_type=pl.DeviceIdType.MESH)

    def others(count, act):
        for index in range(count):
            @pl.when(rep != index)
            def _():
                act(index)

    mean_grad = jnp.zeros((QUADS * T, 1), F32)
    mean_proj = jnp.zeros((QUADS * T, 1), F32)
    arrived(0, cot_send, cot_got, PIECES)
    sent = 0
    for piece, (first, width) in enumerate(z.cuts):
        pick = onehot(code_col == row_ref[piece:piece + 1, :].astype(F32))
        upstream = gather_block(cot_got, pick, first, width, functools.partial(arrived, 0, cot_send, cot_got, piece))
        normed = norm[:, first:first + width]
        product = upstream * normed
        scale = params(gain_ref, first, width)
        scaled = upstream * scale
        ups[:, first:first + width] = scaled
        mean_grad = mean_grad + jnp.sum(scaled, axis=1, keepdims=True)
        mean_proj = mean_proj + jnp.sum(scaled * normed, axis=1, keepdims=True)
        part[:, first:first + width] = jnp.concatenate(
            [jnp.sum(value[quad * T:(quad + 1) * T], axis=0, keepdims=True)
             for value in (product, upstream) for quad in range(QUADS)], axis=0)
        done = (first + width) // LANES
        if sent == 0:
            @pl.when(rank < N - 1)
            def _():
                pl.semaphore_wait(here_rep, N - 1 - rank)
        for tile in range(sent, done):
            slot, index = tile // N, (tile - 1) % N

            @pl.when(rep != index)
            def _():
                reduce_copy(tile, rep).start()

            @pl.when(rep == index)
            def _():
                part_in[index, :, slot * LANES:(slot + 1) * LANES] = part[:, tile * LANES:(tile + 1) * LANES]
        sent = done

    @holding
    def _(count):
        at = slice(0, count * LANES)
        for slot in range(count):
            others(N, lambda index: reduce_copy(slot * N, index).wait_recv())
        total = part_in[0, :, at]
        for index in range(1, N):
            total = total + part_in[index, :, at]
        mid[:, at] = total
        for d in order[::-1]:
            exchange_copy(d, count).start()
        mid_in[pl.ds(me, 1), :, at] = total[None]

    start(1, vis_send, vis_got, *late)

    mean_grad = spread(by_token(mean_grad) / features)
    mean_proj = spread(by_token(mean_proj) / features)
    for first, width in z.cuts:
        grad = inverse * (ups[:, first:first + width] - mean_grad - norm[:, first:first + width] * mean_proj)
        grad_ref[:, first:first + width] = dot(back_ref[...], grad.astype(BF16)).astype(BF16)

    @holding
    def _(count):
        at = slice(0, count * LANES)
        for d in order:
            exchange_copy(d, count).wait()
        total = mid_in[0, :, at]
        for index in range(1, G):
            total = total + mid_in[index, :, at]
        mid[:, at] = total * factor
        others(N, lambda index: gather_copy(index, rep, count).start())
        fin[pl.ds(rep, 1), :, at] = (total * factor)[None]

    def sends_done(which, source, target, chosen):
        for piece in chosen:
            if piece in pieces[which]:
                for d in order:
                    remote(which, source, target, piece, exclusive(me, d, G), me).wait_send()

    def settle():
        for tile in range(z.tiles):
            @pl.when(rep != (tile - 1) % N)
            def _():
                reduce_copy(tile, rep).wait_send()

        @holding
        def _(count):
            others(N, lambda index: gather_copy(index, rep, count).wait_send())

        sends_done(0, cot_send, cot_got, list(range(count)) + [PIECES])
        sends_done(1, vis_send, vis_got, early + [PIECES])

    slot_code = lax.broadcasted_iota(jnp.int32, (z.padded_slots, 1), 0) * QUADS
    code = jnp.concatenate([slot_code + quad for quad in range(QUADS)], axis=0)
    arrived(1, vis_send, vis_got, PIECES)
    for piece in early + late:
        first, width = z.cuts[piece]
        if piece == late[-1]:
            others(N, lambda index: held(index) and gather_copy(0, index, held(index)).wait_recv())
            for quad in range(QUADS):
                for tile in range(z.tiles):
                    index, at = (tile - 1) % N, tile // N * LANES
                    row = quad * z.tiles + tile
                    gain_out[row:row + 1, :] = fin[index, quad:quad + 1, at:at + LANES]
                    bias_out[row:row + 1, :] = fin[index, QUADS + quad:QUADS + quad + 1, at:at + LANES]
            settle()
        pick = onehot(code == row_ref[piece:piece + 1, :])
        block = gather_block(
            vis_got, pick, first, width, functools.partial(arrived, 1, vis_send, vis_got, piece)).astype(BF16)
        for quad in range(QUADS):
            at = quad * z.padded_slots
            visual[:, quad * C + first:quad * C + first + width] = block[at:at + z.slots]
    sends_done(1, vis_send, vis_got, late)


def place_kernel(*refs):
    count = (len(refs) - 1) // 2
    moves = [pltpu.make_async_copy(refs[n], refs[count + n], refs[-1].at[n]) for n in range(count)]
    for move in moves:
        move.start()
    for move in moves:
        move.wait()


def body(encoder_out, destination, norm_gain, norm_bias, cotangent):
    groups, reps = lax.axis_size("enc"), lax.axis_size("rep")
    z = Sizes(encoder_out.shape, cotangent.shape, groups, reps)
    factor = 1.0 / math.sqrt(z.tokens * groups * reps)
    codes = z.codes()
    permutation = z.permutation()
    features = QUADS * z.channels
    rest_rows = max(z.rest_rows, 16)
    block_a, block_b = (groups, max(z.whole, 16), z.channels), (groups, rest_rows, z.width)
    vmem = pl.BlockSpec(memory_space=pltpu.VMEM)
    dma = pltpu.SemaphoreType.DMA
    share = (QUADS * 2, z.share)
    anywhere = pl.BlockSpec(memory_space=pl.ANY)
    rows = features // LANES
    table = jnp.asarray(codes)
    small = [
        pltpu.VMEM((1, z.tokens), jnp.int32),
        pltpu.VMEM((rows, LANES), F32),
        pltpu.VMEM((rows, LANES), F32),
        pltpu.VMEM(permutation.shape, BF16),
        pltpu.VMEM(permutation.shape, BF16),
        pltpu.VMEM(codes.T.shape, jnp.int32),
        pltpu.VMEM(codes.shape, jnp.int32),
    ]
    results = pl.pallas_call(
        functools.partial(kernel, z, factor),
        out_shape=(
            pltpu.VMEM((z.slots, features), BF16),
            pltpu.VMEM((z.patches, z.channels), BF16),
            pltpu.VMEM((rows, LANES), F32),
            pltpu.VMEM((rows, LANES), F32),
        ),
        in_specs=[anywhere] * 9,
        out_specs=(vmem,) * 4,
        scratch_shapes=small + [
            pltpu.VMEM((z.patches, z.channels), BF16),
            pltpu.VMEM((z.slots, features), BF16),
        ]
        + [pltpu.VMEM(shape, BF16) for shape in (block_a, block_b) * 4]
        + [
            pltpu.VMEM((z.patches, z.channels), F32),
            pltpu.VMEM((z.patches, z.channels), F32),
            pltpu.VMEM((QUADS * 2, z.channels), F32),
            pltpu.VMEM((reps,) + share, F32),
            pltpu.VMEM(share, F32),
            pltpu.VMEM((groups,) + share, F32),
            pltpu.VMEM((reps,) + share, F32),
            pltpu.SemaphoreType.REGULAR((groups,)),
            pltpu.SemaphoreType.REGULAR,
            dma((len(small),)),
            dma((2, QUADS)),
            dma,
            dma((2, PIECES + 1, groups)),
            dma((2, PIECES + 1, groups)),
            dma((2, PIECES + 1)),
            dma((z.tiles,)),
            dma((-(-z.tiles // reps), reps)),
            dma((groups,)),
            dma((groups,)),
            dma((reps,)),
            dma((reps,)),
        ],
        compiler_params=pltpu.CompilerParams(collective_id=0, has_side_effects=True, vmem_limit_bytes=60 * 1024 * 1024),
        name="dispatch",
    )(
        encoder_out.reshape(z.patches, z.channels),
        destination.reshape(1, z.tokens),
        norm_gain.reshape(rows, LANES),
        norm_bias.reshape(rows, LANES),
        cotangent,
        jnp.asarray(permutation, BF16),
        jnp.asarray(permutation.T, BF16),
        jnp.asarray(np.ascontiguousarray(codes.T)),
        table,
    )
    visual, grad, gain_sum, bias_sum = pl.pallas_call(
        place_kernel,
        out_shape=tuple(jax.ShapeDtypeStruct(result.shape, result.dtype) for result in results),
        in_specs=[vmem] * 4,
        out_specs=(anywhere,) * 4,
        scratch_shapes=[dma((4,))],
        compiler_params=pltpu.CompilerParams(vmem_limit_bytes=16 * 1024 * 1024),
        name="place",
    )(*results)
    return (visual, grad.reshape(encoder_out.shape), gain_sum.reshape(features), bias_sum.reshape(features))


def solution(mesh):
    placed = (
        P(("enc", "rep"), None, None),
        P(("enc", "rep"), None),
        P(),
        P(),
        P(("enc", "rep"), None),
    )
    return jax.shard_map(
        body,
        mesh=mesh,
        in_specs=placed,
        out_specs=(P(("enc", "rep"), None), P(("enc", "rep"), None, None), P(), P()),
        check_vma=False,
    )
```
